256 devices in a mesh: seq: 64 (over z, y, core), tp: 4 (over x).
Axes of the slice: x: 4, y: 4, z: 8, core: 2. Of those that a mesh axis runs over, the one named last changes fastest.
Arguments:
- probe_vectors: bfloat16 [32768, 8192], P('seq', 'tp'), may hold values from -6 to 6
- lookup_vectors: bfloat16 [32768, 8192], P('seq', 'tp'), may hold values from -0.5 to 0.5
- payload_vectors: bfloat16 [32768, 8192], P('seq', 'tp'), may hold values from -400 to 400
- attender_fading_pace: float32 [64], P('tp'), may hold values from 0 to 0.034, as said below
- surplus_fading: float32 [32768, 64], P('seq', 'tp'), may hold values from -0.7 to 0, as said below
- normalizer_scaling: float32 [8192], P('tp'), may hold values from 0.25 to 1.75
Outputs:
- attended: bfloat16 [32768, 8192], P('seq', 'tp')
- final_state: float32 [64, 16384], P('tp', 'seq')
The draws below stay inside these ranges and needn't reach their ends.
Inputs may be any that keep to these rules, and one draw needn't show every extreme that they name: `attender_fading_pace`: positive per-token decay rates; some heads forget within some tens of tokens. `surplus_fading`: zero at most tokens.
All inputs are finite; a program needn't handle non-finite values.
Results may differ from the reference program's by a relative error of at most 0.0031.
Values sent between devices are 32-bit elements; how exact they have to be, the bound alone decides.
No kernel may reach another device: no remote copies, remote signals or barrier semaphores. Data moves between devices by JAX's collectives and lax.ppermute only.
A program may use at most 192 MiB of HBM per device.

```python
import math
import jax
import jax.numpy as jnp
from jax import lax

HEADS = 64
HEAD_DIM = 128
BLOCK = 256
D = 8192
TOKENS = 32768


def draw_payload_vectors(key, part):
    first, second_operand = jax.random.split(key, 2)
    base = jnp.clip(jax.random.normal(first, (TOKENS, D), jnp.float32), -4.0, 4.0)
    column = jnp.exp(jax.random.uniform(second_operand, (1, D), jnp.float32, 0.0, math.log(10.0)))
    return (base * column).astype(jnp.bfloat16)


def draw_attender_fading_pace(key, part):
    key_choice, key_slow, key_medium, key_fast, key_quick = jax.random.split(key, 5)
    slow_share = 0.5
    medium_share = 0.65
    fast_share = 0.88
    picker = jax.random.uniform(key_choice, (HEADS,), jnp.float32)
    slow_rates = jnp.exp(jax.random.uniform(key_slow, (HEADS,), jnp.float32, math.log(0.05), math.log(0.8))) / TOKENS
    medium_rates = jnp.exp(jax.random.uniform(key_medium, (HEADS,), jnp.float32, math.log(0.0002), math.log(0.00039)))
    fast_rates = jax.random.uniform(key_fast, (HEADS,), jnp.float32, 0.0098, 0.0125)
    quick_rates = jnp.exp(jax.random.uniform(key_quick, (HEADS,), jnp.float32, math.log(1.0 / 50.0), math.log(1.0 / 30.0)))
    rates = jnp.where(picker < slow_share, slow_rates, jnp.where(picker < medium_share, medium_rates, jnp.where(picker < fast_share, fast_rates, quick_rates)))
    return rates.astype(jnp.float32)


def draw_surplus_fading(key, part):
    first, second_operand = jax.random.split(key, 2)
    hits = jax.random.uniform(first, (TOKENS, HEADS), jnp.float32) < 2.0 / TOKENS
    depth = jnp.log(jax.random.uniform(second_operand, (TOKENS, HEADS), jnp.float32, 0.5, 0.8))
    return jnp.where(hits, depth, 0.0).astype(jnp.float32)


def block_levels(stream_key, dims, shards, low, top_value):
    factor_of = 1.0
    for axis_at, parts in shards:
        draws = jax.random.uniform(jax.random.fold_in(jax.random.fold_in(stream_key, 6), axis_at), (parts,), jnp.float32, low / len(shards), top_value / len(shards))
        factor_of = factor_of * jnp.repeat(jnp.exp(draws), dims[axis_at] // parts).reshape((-1,) + (1,) * (len(dims) - 1 - axis_at))
    return factor_of


def normal_values(own_key, extent, width, limit, pieces=(), held_as=jnp.bfloat16):
    result = width * jax.random.normal(own_key, extent, jnp.float32)
    if pieces:
        result = result * block_levels(own_key, extent, pieces, -0.22, 0.18)
    return jnp.clip(result, -limit, limit).astype(held_as)


def setup_inputs(seed: int = 0) -> dict:
    seeds = jax.random.split(jax.random.key(seed), 7)
    probe_vectors = normal_values(seeds[0], (TOKENS, D), 1.0, 6.0, ((0, 64), (1, 4)))
    lookup_vectors = normal_values(seeds[1], (TOKENS, D), HEAD_DIM ** -0.5, 0.5, ((0, 64), (1, 4)))
    payload_vectors = draw_payload_vectors(jax.random.fold_in(seeds[6], 71), 0)
    attender_fading_pace = draw_attender_fading_pace(jax.random.fold_in(seeds[6], 71), 0)
    surplus_fading = draw_surplus_fading(jax.random.fold_in(seeds[6], 71), 0)
    normalizer_scaling = jnp.clip(1.0 + 0.15 * jax.random.normal(seeds[5], (D,), jnp.float32), 0.25, 1.75)
    return {"probe_vectors": probe_vectors, "lookup_vectors": lookup_vectors, "payload_vectors": payload_vectors, "attender_fading_pace": attender_fading_pace, "surplus_fading": surplus_fading, "normalizer_scaling": normalizer_scaling}


def block_update(qb, kb, vb, gb, state):
    c = jnp.cumsum(gb, axis=0)
    qf = qb.astype(jnp.float32)
    kf = kb.astype(jnp.float32)
    vf = vb.astype(jnp.float32)
    scores = jnp.einsum('thd,shd->hts', qf, kf, precision=lax.Precision.HIGHEST)
    trans = c.T
    diff = trans[:, :, None] - trans[:, None, :]
    size = c.shape[0]
    lower = jnp.arange(size)[:, None] >= jnp.arange(size)[None, :]
    factor = jnp.where(lower[None, :, :], jnp.exp(jnp.minimum(diff, 0.0)), 0.0)
    rounded = lax.optimization_barrier((scores * factor).astype(jnp.bfloat16)).astype(jnp.float32)
    intra = jnp.einsum('hts,shd->thd', rounded, vf, precision=lax.Precision.HIGHEST)
    inter = jnp.exp(c)[:, :, None] * jnp.einsum('thd,hde->the', qf, state, precision=lax.Precision.HIGHEST)
    last = c[-1]
    decayed = kf * jnp.exp(last[None, :] - c)[:, :, None]
    fresh = jnp.exp(last)[:, None, None] * state + jnp.einsum('thd,the->hde', decayed, vf, precision=lax.Precision.HIGHEST)
    return (intra + inter, fresh)

def reference(probe_vectors, lookup_vectors, payload_vectors, attender_fading_pace, surplus_fading, normalizer_scaling):
    block_list = TOKENS // BLOCK
    exponent_of_fading = surplus_fading - attender_fading_pace[None, :]
    shaped = lambda arr: arr.reshape(block_list, BLOCK, HEADS, HEAD_DIM)

    def step(state, input_arrays):
        qb, kb, vb, gb = input_arrays
        out, fresh = block_update(qb, kb, vb, gb, state)
        return (fresh, out)
    start = jnp.zeros((HEADS, HEAD_DIM, HEAD_DIM), jnp.float32)
    final, outs = lax.scan(step, start, (shaped(probe_vectors), shaped(lookup_vectors), shaped(payload_vectors), exponent_of_fading.reshape(block_list, BLOCK, HEADS)))
    merged = outs.reshape(TOKENS, D)
    meansq = lax.optimization_barrier(jnp.sum(merged * merged, axis=1, keepdims=True)) / D
    attended = (merged * lax.rsqrt(meansq + 1e-06) * normalizer_scaling[None, :]).astype(jnp.bfloat16)
    return (attended, final.reshape(HEADS, HEAD_DIM * HEAD_DIM))
```

```python
import functools

import jax
import jax.numpy as jnp
from jax import lax
from jax.experimental import pallas as pl
from jax.experimental.pallas import tpu as pltpu
from jax.sharding import Mesh
from jax.sharding import PartitionSpec as P

HEAD_DIM = 128
BLOCK = 256
D = 8192
SEQ = ("seq_0", "seq_1", "seq_2")
CHIPS = ("seq_0", "seq_1")
CORE = "seq_2"
HEADS_HERE = 16
TOKENS_HERE = 512
GROUP = 4
GROUPS = HEADS_HERE // GROUP
CHIP_COUNT = 32
PIECE = 32
F32 = jnp.float32
BF16 = jnp.bfloat16


def dot(a, b, dims=((1,), (0,))):
    return lax.dot_general(a, b, (dims, ((), ())), preferred_element_type=F32)


def split(x):
    high = x.astype(BF16)
    return high, (x - high.astype(F32)).astype(BF16)


def log_decay(fading, pace):
    heads, tokens = fading.shape
    row = lax.broadcasted_iota(jnp.int32, (heads, heads), 0)
    col = lax.broadcasted_iota(jnp.int32, (heads, heads), 1)
    pace_column = jnp.sum(
        jnp.where(row == col, jnp.broadcast_to(pace, (heads, heads)), 0.0), axis=1, keepdims=True
    )
    c = fading - pace_column
    lane = lax.broadcasted_iota(jnp.int32, (heads, tokens), 1)
    shift = 1
    while shift < tokens:
        c = c + jnp.where(lane >= shift, pltpu.roll(c, shift, axis=1), 0.0)
        shift *= 2
    return c


def to_columns(rows):
    heads, tokens = rows.shape
    full = jnp.concatenate([rows, jnp.zeros((128 - heads, tokens), F32)], axis=0)
    return full.T


def total_row(c):
    heads = c.shape[0]
    last = jnp.broadcast_to(c[:, -1:], (heads, 128))
    row = lax.broadcasted_iota(jnp.int32, (heads, 128), 0)
    lane = lax.broadcasted_iota(jnp.int32, (heads, 128), 1)
    return jnp.sum(jnp.where(row == lane, last, 0.0), axis=0, keepdims=True)


def piece_column(row):
    r = lax.broadcasted_iota(jnp.int32, (PIECE, 128), 0)
    lane = lax.broadcasted_iota(jnp.int32, (PIECE, 128), 1)
    picked = jnp.where(lane == r // 2, jnp.broadcast_to(row, (PIECE, 128)), 0.0)
    return jnp.broadcast_to(jnp.sum(picked, axis=1, keepdims=True), (PIECE, 128))


def shuffle(x):
    sub = lax.broadcasted_iota(jnp.int32, x[0].shape, 1)
    for step in (1, 2):
        upper = ((sub // 2) & step) != 0
        y = list(x)
        for a in range(4):
            if a & step:
                continue
            b = a + step
            y[a] = jnp.where(upper, pltpu.roll(x[b], 2 * step, axis=1), x[a])
            y[b] = jnp.where(upper, x[b], pltpu.roll(x[a], 8 - 2 * step, axis=1))
        x = y
    return x


def state_kernel(k_ref, v_ref, fading_ref, pace_ref, keep_ref, send_ref, whole_ref, w_ref):
    g = pl.program_id(0)
    mine = lax.axis_index(CORE)

    @pl.when(g == 0)
    def _():
        c = log_decay(fading_ref[...], pace_ref[...])
        w_ref[...] = jnp.exp(c[:, -1:] - c)
        total = jnp.broadcast_to(total_row(c), (8, 128))
        keep_ref[pl.ds(CHIP_COUNT * PIECE, 8), :] = total
        send_ref[pl.ds(CHIP_COUNT * PIECE, 8), :] = total

    states = []
    for i in range(GROUP):
        lanes = slice(i * HEAD_DIM, (i + 1) * HEAD_DIM)
        turned = k_ref[:, lanes].T.astype(F32)
        decayed = turned * w_ref[pl.ds(g * GROUP + i, 1), :]
        high, low = split(decayed)
        both = dot(jnp.concatenate([high, low], axis=0), v_ref[:, lanes])
        state = both[:HEAD_DIM] + both[HEAD_DIM:]
        whole_ref[i] = state
        states.append(state.reshape(16, 8, 128))
    units = shuffle(states)
    for b in range(2):
        even, odd = units[2 * b], units[2 * b + 1]
        kept = jnp.where(mine == 0, even, odd)
        sent = jnp.where(mine == 0, odd, even)
        for j in range(16):
            at = pl.ds(pl.multiple_of((2 * j + b) * PIECE + g * 8, 8), 8)
            keep_ref[at, :] = kept[j]
            send_ref[at, :] = sent[j]


def local_states(k, v, fading, pace):
    rows = CHIP_COUNT * PIECE + 8
    return pl.pallas_call(
        state_kernel,
        grid=(GROUPS,),
        in_specs=[
            pl.BlockSpec((TOKENS_HERE, GROUP * HEAD_DIM), lambda g: (0, g)),
            pl.BlockSpec((TOKENS_HERE, GROUP * HEAD_DIM), lambda g: (0, g)),
            pl.BlockSpec((HEADS_HERE, TOKENS_HERE), lambda g: (0, 0)),
            pl.BlockSpec((1, HEADS_HERE), lambda g: (0, 0)),
        ],
        out_specs=[
            pl.BlockSpec((rows, 128), lambda g: (0, 0)),
            pl.BlockSpec((rows, 128), lambda g: (0, 0)),
            pl.BlockSpec((GROUP, HEAD_DIM, HEAD_DIM), lambda g: (g, 0, 0)),
        ],
        out_shape=[
            jax.ShapeDtypeStruct((rows, 128), F32),
            jax.ShapeDtypeStruct((rows, 128), F32),
            jax.ShapeDtypeStruct((HEADS_HERE, HEAD_DIM, HEAD_DIM), F32),
        ],
        scratch_shapes=[pltpu.VMEM((HEADS_HERE, TOKENS_HERE), F32)],
        compiler_params=pltpu.CompilerParams(vmem_limit_bytes=24 << 20),
        cost_estimate=pl.CostEstimate(flops=600_000_000, bytes_accessed=6 << 20, transcendentals=8192),
        name="local_states",
    )(k, v, fading, pace)


def chip_kernel(own_ref, other_ref, out_ref):
    mine = lax.axis_index(CORE)
    tail = pl.ds(CHIP_COUNT * PIECE, 1)
    own_total, other_total = own_ref[tail, :], other_ref[tail, :]
    later = piece_column(jnp.exp(jnp.where(mine == 0, other_total, own_total)))
    own_factor = jnp.where(mine == 0, later, 1.0)
    other_factor = jnp.where(mine == 0, 1.0, later)
    total = own_total + other_total
    for p in range(CHIP_COUNT):
        at = pl.ds(p * PIECE, PIECE)
        out_ref[pl.ds(p * (PIECE + 1), PIECE), :] = (
            own_factor * own_ref[at, :] + other_factor * other_ref[at, :]
        )
        out_ref[pl.ds(p * (PIECE + 1) + PIECE, 1), :] = total


def chip_states(own, other):
    return pl.pallas_call(
        chip_kernel,
        out_shape=jax.ShapeDtypeStruct((CHIP_COUNT * (PIECE + 1), 128), F32),
        compiler_params=pltpu.CompilerParams(vmem_limit_bytes=8 << 20),
        cost_estimate=pl.CostEstimate(flops=1 << 19, bytes_accessed=3 << 19, transcendentals=128),
        name="chip_states",
    )(own, other)


def scan_kernel(in_ref, _, out_ref, final_ref, last_ref):
    state = jnp.zeros((PIECE, 128), F32)
    for p in range(CHIP_COUNT):
        out_ref[pl.ds(p * PIECE, PIECE), :] = state
        factor = piece_column(jnp.exp(in_ref[pl.ds(p * (PIECE + 1) + PIECE, 1), :]))
        state = factor * state + in_ref[pl.ds(p * (PIECE + 1), PIECE), :]
    last_ref[...] = state
    for i in range(2):
        final_ref[:, i * 128 : (i + 1) * 128] = last_ref[pl.ds(i, HEADS_HERE, stride=2), :]


def scan_chips(pieces, after):
    return pl.pallas_call(
        scan_kernel,
        out_shape=[
            jax.ShapeDtypeStruct((CHIP_COUNT * PIECE, 128), F32),
            jax.ShapeDtypeStruct((HEADS_HERE, 2 * HEAD_DIM), F32),
        ],
        scratch_shapes=[pltpu.VMEM((PIECE, 128), F32)],
        compiler_params=pltpu.CompilerParams(vmem_limit_bytes=8 << 20),
        cost_estimate=pl.CostEstimate(flops=1 << 19, bytes_accessed=1 << 20, transcendentals=4096),
        name="scan_chips",
    )(pieces, after)


def inside_kernel(q_ref, k_ref, v_ref, fading_ref, pace_ref, start_ref, out_ref, token_ref, c_ref, column_ref):
    g = pl.program_id(0)

    @pl.when(g == 0)
    def _():
        c = log_decay(fading_ref[...], pace_ref[...])
        c_ref[...] = c
        column_ref[...] = to_columns(c)
        token_ref[...] = jnp.zeros_like(token_ref)

    columns = pltpu.roll(column_ref[...], lax.rem(128 - g * GROUP, 128), axis=1)
    row = lax.broadcasted_iota(jnp.int32, (BLOCK, BLOCK), 0)
    col = lax.broadcasted_iota(jnp.int32, (BLOCK, BLOCK), 1)
    for i in range(GROUP):
        lanes = slice(i * HEAD_DIM, (i + 1) * HEAD_DIM)
        c_row = c_ref[pl.ds(g * GROUP + i, 1), :]
        state = start_ref[i]
        base = jnp.zeros((1, 1), F32)
        for b in range(TOKENS_HERE // BLOCK):
            rows = slice(b * BLOCK, (b + 1) * BLOCK)
            q, k, v = q_ref[rows, lanes], k_ref[rows, lanes], v_ref[rows, lanes]
            c_here = c_row[:, rows]
            c_column = columns[rows, i : i + 1]
            diff = c_column - c_here
            factor = jnp.where(row >= col, jnp.exp(jnp.minimum(diff, 0.0)), 0.0)
            weights = (dot(q, k, ((1,), (1,))) * factor).astype(BF16)
            high, low = split(state)
            carried = dot(q, high) + dot(q, low)
            out_ref[rows, lanes] = dot(weights, v) + jnp.exp(c_column - base) * carried
            if b + 1 < TOKENS_HERE // BLOCK:
                last = c_here[:, -1:]
                decayed = k.T.astype(F32) * jnp.exp(last - c_here)
                high, low = split(decayed)
                state = jnp.exp(last - base) * state + dot(high, v) + dot(low, v)
                base = last


def inside(q, k, v, fading, pace, start):
    wide = pl.BlockSpec((TOKENS_HERE, GROUP * HEAD_DIM), lambda g: (0, g))
    return pl.pallas_call(
        inside_kernel,
        grid=(GROUPS,),
        in_specs=[
            wide,
            wide,
            wide,
            pl.BlockSpec((HEADS_HERE, TOKENS_HERE), lambda g: (0, 0)),
            pl.BlockSpec((1, HEADS_HERE), lambda g: (0, 0)),
            pl.BlockSpec((GROUP, HEAD_DIM, HEAD_DIM), lambda g: (g, 0, 0)),
        ],
        out_specs=[wide, pl.BlockSpec((8, 128), lambda g: (0, 0))],
        out_shape=[
            jax.ShapeDtypeStruct((TOKENS_HERE, HEADS_HERE * HEAD_DIM), F32),
            jax.ShapeDtypeStruct((8, 128), F32),
        ],
        scratch_shapes=[
            pltpu.VMEM((HEADS_HERE, TOKENS_HERE), F32),
            pltpu.VMEM((TOKENS_HERE, 128), F32),
        ],
        compiler_params=pltpu.CompilerParams(vmem_limit_bytes=24 << 20),
        cost_estimate=pl.CostEstimate(
            flops=2_000_000_000, bytes_accessed=11 << 20, transcendentals=2 << 20
        ),
        name="inside",
    )(q, k, v, fading, pace, start)


def outside_kernel(
    q_ref, before_ref, own_ref, other_ref, tail_ref, fading_ref, pace_ref, out_ref, squares_ref, column_ref, sum_ref
):
    g = pl.program_id(0)
    mine = lax.axis_index(CORE)

    @pl.when(g == 0)
    def _():
        c = log_decay(fading_ref[...], pace_ref[...])
        partner = jnp.where(mine == 0, 0.0, tail_ref[0:1, :])
        column_ref[...] = jnp.exp(to_columns(c) + partner)
        sum_ref[...] = jnp.zeros_like(sum_ref)

    columns = pltpu.roll(column_ref[...], lax.rem(128 - g * GROUP, 128), axis=1)
    own, other = own_ref[...], other_ref[...]
    even = jnp.where(mine == 0, own, other).reshape(16, 2, 8, 128)
    odd = jnp.where(mine == 0, other, own).reshape(16, 2, 8, 128)
    states = shuffle([even[:, 0], odd[:, 0], even[:, 1], odd[:, 1]])
    total = sum_ref[...]
    for i in range(GROUP):
        lanes = slice(i * HEAD_DIM, (i + 1) * HEAD_DIM)
        high, low = split(states[i].reshape(HEAD_DIM, HEAD_DIM))
        q = q_ref[:, lanes]
        out = before_ref[:, lanes] + columns[:, i : i + 1] * (dot(q, high) + dot(q, low))
        out_ref[:, lanes] = out
        total = total + out * out
    sum_ref[...] = total

    @pl.when(g == GROUPS - 1)
    def _():
        squares_ref[...] = jnp.sum(total.T, axis=0, keepdims=True)


def outside(q, before, own, other, received, fading, pace):
    wide = pl.BlockSpec((TOKENS_HERE, GROUP * HEAD_DIM), lambda g: (0, g))
    pieces = pl.BlockSpec((CHIP_COUNT, 8, 128), lambda g: (0, g, 0))
    return pl.pallas_call(
        outside_kernel,
        grid=(GROUPS,),
        in_specs=[
            wide,
            wide,
            pieces,
            pieces,
            pl.BlockSpec((8, 128), lambda g: (CHIP_COUNT * PIECE // 8, 0)),
            pl.BlockSpec((HEADS_HERE, TOKENS_HERE), lambda g: (0, 0)),
            pl.BlockSpec((1, HEADS_HERE), lambda g: (0, 0)),
        ],
        out_specs=[wide, pl.BlockSpec((1, TOKENS_HERE), lambda g: (0, 0))],
        out_shape=[
            jax.ShapeDtypeStruct((TOKENS_HERE, HEADS_HERE * HEAD_DIM), F32),
            jax.ShapeDtypeStruct((1, TOKENS_HERE), F32),
        ],
        scratch_shapes=[
            pltpu.VMEM((TOKENS_HERE, 128), F32),
            pltpu.VMEM((TOKENS_HERE, 128), F32),
        ],
        compiler_params=pltpu.CompilerParams(vmem_limit_bytes=24 << 20),
        cost_estimate=pl.CostEstimate(
            flops=600_000_000, bytes_accessed=11 << 20, transcendentals=1 << 16
        ),
        name="outside",
    )(q, before, own, other, received, fading, pace)


def norm_kernel(out_ref, *refs):
    *square_refs, gain_ref, result_ref = refs
    rows = out_ref.shape[0]
    total = sum(ref[...] for ref in square_refs)
    scale = lax.rsqrt(total / D + 1e-06)
    column = jnp.broadcast_to(scale, (128, rows)).T
    for h in range(HEADS_HERE):
        lanes = slice(h * HEAD_DIM, (h + 1) * HEAD_DIM)
        result_ref[:, lanes] = (out_ref[:, lanes] * column * gain_ref[:, lanes]).astype(BF16)


def normed(out, squares, gain):
    rows = 128
    width = HEADS_HERE * HEAD_DIM
    return pl.pallas_call(
        norm_kernel,
        grid=(TOKENS_HERE // rows,),
        in_specs=[
            pl.BlockSpec((rows, width), lambda t: (t, 0)),
            *(pl.BlockSpec((1, rows), lambda t: (0, t)) for _ in squares),
            pl.BlockSpec((1, width), lambda t: (0, 0)),
        ],
        out_specs=pl.BlockSpec((rows, width), lambda t: (t, 0)),
        out_shape=jax.ShapeDtypeStruct((TOKENS_HERE, width), BF16),
        compiler_params=pltpu.CompilerParams(vmem_limit_bytes=24 << 20),
        cost_estimate=pl.CostEstimate(flops=1 << 21, bytes_accessed=6 << 20, transcendentals=512),
        name="normed",
    )(out, *squares, gain)


def turned(value, by):
    count = lax.axis_size("tp")
    return lax.ppermute(value, "tp", [((i + by) % count, i) for i in range(count)])


def on_device(q, k, v, pace, fading, gain):
    q, k, v, fading, pace = (
        pltpu.with_memory_space_constraint(part, pltpu.HBM)
        for part in (q, k, v, fading.T, pace.reshape(1, HEADS_HERE))
    )
    keep, send, whole = local_states(k, v, fading, pace)
    swap = [(0, 1), (1, 0)]
    received = lax.ppermute(send, CORE, swap)
    chip = chip_states(keep, received)
    gathered = lax.all_to_all(
        chip.reshape(CHIP_COUNT, PIECE + 1, 1, 128), CHIPS, 0, 0, tiled=True
    )
    start = lax.ppermute(whole, CORE, [(0, 1)])
    before, token = inside(q, k, v, fading, pace, start)
    before = pltpu.with_memory_space_constraint(before, pltpu.HBM)
    prior, final = scan_chips(gathered.reshape(CHIP_COUNT * (PIECE + 1), 128), token)
    own = lax.all_to_all(prior.reshape(CHIP_COUNT, PIECE, 128), CHIPS, 0, 0, tiled=True)
    other = lax.ppermute(own, CORE, swap)
    out, squares = outside(q, before, own, other, received, fading, pace)
    squares = [squares, *(turned(squares, by) for by in (1, 3, 2))]
    return normed(out, squares, gain.reshape(1, -1)), final


def solution(mesh):
    split_mesh = Mesh(
        mesh.devices.reshape(8, 4, 2, mesh.shape["tp"]), ("seq_0", "seq_1", "seq_2", "tp")
    )
    return jax.shard_map(
        on_device,
        mesh=split_mesh,
        in_specs=(P(SEQ, "tp"), P(SEQ, "tp"), P(SEQ, "tp"), P("tp"), P(SEQ, "tp"), P("tp")),
        out_specs=(P(SEQ, "tp"), P("tp", SEQ)),
        check_vma=False,
    )
```

```python
import functools

import jax
import jax.numpy as jnp
from jax import lax
from jax.experimental import pallas as pl
from jax.experimental.pallas import tpu as pltpu
from jax.sharding import Mesh
from jax.sharding import PartitionSpec as P

HEAD_DIM = 128
BLOCK = 256
D = 8192
SEQ = ("seq_0", "seq_1", "seq_2")
CHIPS = ("seq_0", "seq_1")
CORE = "seq_2"
HEADS_HERE = 16
TOKENS_HERE = 512
GROUP = 4
GROUPS = HEADS_HERE // GROUP
CHIP_COUNT = 32
PIECE = 32
F32 = jnp.float32
BF16 = jnp.bfloat16


def dot(a, b, dims=((1,), (0,))):
    return lax.dot_general(a, b, (dims, ((), ())), preferred_element_type=F32)


def split(x):
    high = x.astype(BF16)
    return high, (x - high.astype(F32)).astype(BF16)


def log_decay(fading, pace):
    heads, tokens = fading.shape
    row = lax.broadcasted_iota(jnp.int32, (heads, heads), 0)
    col = lax.broadcasted_iota(jnp.int32, (heads, heads), 1)
    pace_column = jnp.sum(
        jnp.where(row == col, jnp.broadcast_to(pace, (heads, heads)), 0.0), axis=1, keepdims=True
    )
    c = fading - pace_column
    lane = lax.broadcasted_iota(jnp.int32, (heads, tokens), 1)
    shift = 1
    while shift < tokens:
        c = c + jnp.where(lane >= shift, pltpu.roll(c, shift, axis=1), 0.0)
        shift *= 2
    return c


def to_columns(rows):
    heads, tokens = rows.shape
    full = jnp.concatenate([rows, jnp.zeros((128 - heads, tokens), F32)], axis=0)
    return full.T


def total_row(c):
    heads = c.shape[0]
    last = jnp.broadcast_to(c[:, -1:], (heads, 128))
    row = lax.broadcasted_iota(jnp.int32, (heads, 128), 0)
    lane = lax.broadcasted_iota(jnp.int32, (heads, 128), 1)
    return jnp.sum(jnp.where(row == lane, last, 0.0), axis=0, keepdims=True)


def piece_column(row):
    r = lax.broadcasted_iota(jnp.int32, (PIECE, 128), 0)
    lane = lax.broadcasted_iota(jnp.int32, (PIECE, 128), 1)
    picked = jnp.where(lane == r // 2, jnp.broadcast_to(row, (PIECE, 128)), 0.0)
    return jnp.broadcast_to(jnp.sum(picked, axis=1, keepdims=True), (PIECE, 128))


def shuffle(x):
    sub = lax.broadcasted_iota(jnp.int32, x[0].shape, 1)
    for step in (1, 2):
        upper = ((sub // 2) & step) != 0
        y = list(x)
        for a in range(4):
            if a & step:
                continue
            b = a + step
            y[a] = jnp.where(upper, pltpu.roll(x[b], 2 * step, axis=1), x[a])
            y[b] = jnp.where(upper, x[b], pltpu.roll(x[a], 8 - 2 * step, axis=1))
        x = y
    return x


def state_kernel(k_ref, v_ref, fading_ref, pace_ref, keep_ref, send_ref, w_ref):
    g = pl.program_id(0)
    mine = lax.axis_index(CORE)

    @pl.when(g == 0)
    def _():
        c = log_decay(fading_ref[...], pace_ref[...])
        w_ref[...] = jnp.exp(c[:, -1:] - c)
        total = jnp.broadcast_to(total_row(c), (8, 128))
        keep_ref[pl.ds(CHIP_COUNT * PIECE, 8), :] = total
        send_ref[pl.ds(CHIP_COUNT * PIECE, 8), :] = total

    states = []
    for i in range(GROUP):
        lanes = slice(i * HEAD_DIM, (i + 1) * HEAD_DIM)
        turned = k_ref[:, lanes].T.astype(F32)
        decayed = turned * w_ref[pl.ds(g * GROUP + i, 1), :]
        high, low = split(decayed)
        both = dot(jnp.concatenate([high, low], axis=0), v_ref[:, lanes])
        state = both[:HEAD_DIM] + both[HEAD_DIM:]
        states.append(state.reshape(16, 8, 128))
    units = shuffle(states)
    for b in range(2):
        even, odd = units[2 * b], units[2 * b + 1]
        kept = jnp.where(mine == 0, even, odd)
        sent = jnp.where(mine == 0, odd, even)
        for j in range(16):
            at = pl.ds(pl.multiple_of((2 * j + b) * PIECE + g * 8, 8), 8)
            keep_ref[at, :] = kept[j]
            send_ref[at, :] = sent[j]


def local_states(k, v, fading, pace):
    rows = CHIP_COUNT * PIECE + 8
    return pl.pallas_call(
        state_kernel,
        grid=(GROUPS,),
        in_specs=[
            pl.BlockSpec((TOKENS_HERE, GROUP * HEAD_DIM), lambda g: (0, g)),
            pl.BlockSpec((TOKENS_HERE, GROUP * HEAD_DIM), lambda g: (0, g)),
            pl.BlockSpec((HEADS_HERE, TOKENS_HERE), lambda g: (0, 0)),
            pl.BlockSpec((1, HEADS_HERE), lambda g: (0, 0)),
        ],
        out_specs=[
            pl.BlockSpec((rows, 128), lambda g: (0, 0)),
            pl.BlockSpec((rows, 128), lambda g: (0, 0)),
        ],
        out_shape=[
            jax.ShapeDtypeStruct((rows, 128), F32),
            jax.ShapeDtypeStruct((rows, 128), F32),
        ],
        scratch_shapes=[pltpu.VMEM((HEADS_HERE, TOKENS_HERE), F32)],
        compiler_params=pltpu.CompilerParams(vmem_limit_bytes=24 << 20),
        cost_estimate=pl.CostEstimate(flops=600_000_000, bytes_accessed=6 << 20, transcendentals=8192),
        name="local_states",
    )(k, v, fading, pace)


def chip_kernel(own_ref, other_ref, out_ref, _):
    mine = lax.axis_index(CORE)
    tail = pl.ds(CHIP_COUNT * PIECE, 1)
    own_total, other_total = own_ref[tail, :], other_ref[tail, :]
    later = piece_column(jnp.exp(jnp.where(mine == 0, other_total, own_total)))
    own_factor = jnp.where(mine == 0, later, 1.0)
    other_factor = jnp.where(mine == 0, 1.0, later)
    total = own_total + other_total
    for p in range(CHIP_COUNT):
        at = pl.ds(p * PIECE, PIECE)
        out_ref[pl.ds(p * (PIECE + 1), PIECE), :] = (
            own_factor * own_ref[at, :] + other_factor * other_ref[at, :]
        )
        out_ref[pl.ds(p * (PIECE + 1) + PIECE, 1), :] = total


def chip_states(own, other):
    return pl.pallas_call(
        chip_kernel,
        in_specs=[pl.BlockSpec(memory_space=pltpu.VMEM)] * 2,
        out_specs=[pl.BlockSpec(memory_space=pltpu.VMEM)] * 2,
        out_shape=[
            jax.ShapeDtypeStruct((CHIP_COUNT * (PIECE + 1), 128), F32),
            jax.ShapeDtypeStruct(own.shape, F32),
        ],
        input_output_aliases={0: 1},
        compiler_params=pltpu.CompilerParams(vmem_limit_bytes=8 << 20),
        cost_estimate=pl.CostEstimate(flops=1 << 19, bytes_accessed=3 << 19, transcendentals=128),
        name="chip_states",
    )(own, other)


def scan_kernel(in_ref, out_ref, final_ref, last_ref):
    state = jnp.zeros((PIECE, 128), F32)
    for p in range(CHIP_COUNT):
        out_ref[pl.ds(p * PIECE, PIECE), :] = state
        factor = piece_column(jnp.exp(in_ref[pl.ds(p * (PIECE + 1) + PIECE, 1), :]))
        state = factor * state + in_ref[pl.ds(p * (PIECE + 1), PIECE), :]
    last_ref[...] = state
    for i in range(2):
        final_ref[:, i * 128 : (i + 1) * 128] = last_ref[pl.ds(i, HEADS_HERE, stride=2), :]


def scan_chips(pieces):
    return pl.pallas_call(
        scan_kernel,
        out_shape=[
            jax.ShapeDtypeStruct((CHIP_COUNT * PIECE, 128), F32),
            jax.ShapeDtypeStruct((HEADS_HERE, 2 * HEAD_DIM), F32),
        ],
        scratch_shapes=[pltpu.VMEM((PIECE, 128), F32)],
        compiler_params=pltpu.CompilerParams(vmem_limit_bytes=8 << 20),
        cost_estimate=pl.CostEstimate(flops=1 << 19, bytes_accessed=1 << 20, transcendentals=4096),
        name="scan_chips",
    )(pieces)


def inside_kernel(
    first, q_ref, k_ref, v_ref, fading_ref, pace_ref, even_ref, odd_ref, out_ref, *more
):
    *factor_ref, c_ref, column_ref = more
    g = pl.program_id(0)
    h0 = first + g * GROUP
    second = lax.axis_index(CORE) == 1

    @pl.when(g == 0)
    def _():
        c = log_decay(fading_ref[...], pace_ref[...])
        c_ref[...] = c
        column_ref[...] = to_columns(c)
        if factor_ref:
            partner = jnp.where(second, odd_ref[pl.ds(CHIP_COUNT * PIECE, 1), :], 0.0)
            factor_ref[0][...] = jnp.exp(column_ref[...] + partner)

    columns = pltpu.roll(column_ref[...], lax.rem(128 - h0, 128), axis=1)
    starts = shuffle(
        [
            jnp.stack(
                [
                    jnp.where(second, ref[pl.ds(pl.multiple_of((2 * j + b) * PIECE + 2 * h0, 8), 8), :], 0.0)
                    for j in range(16)
                ]
            )
            for b in range(2)
            for ref in (even_ref, odd_ref)
        ]
    )
    row = lax.broadcasted_iota(jnp.int32, (BLOCK, BLOCK), 0)
    col = lax.broadcasted_iota(jnp.int32, (BLOCK, BLOCK), 1)
    for i in range(GROUP):
        lanes = slice(i * HEAD_DIM, (i + 1) * HEAD_DIM)
        c_row = c_ref[pl.ds(h0 + i, 1), :]
        state = starts[i].reshape(HEAD_DIM, HEAD_DIM)
        base = jnp.zeros((1, 1), F32)
        for b in range(TOKENS_HERE // BLOCK):
            rows = slice(b * BLOCK, (b + 1) * BLOCK)
            q, k, v = q_ref[rows, lanes], k_ref[rows, lanes], v_ref[rows, lanes]
            c_here = c_row[:, rows]
            c_column = columns[rows, i : i + 1]
            diff = c_column - c_here
            factor = jnp.where(row >= col, jnp.exp(jnp.minimum(diff, 0.0)), 0.0)
            weights = (dot(q, k, ((1,), (1,))) * factor).astype(BF16)
            high, low = split(state)
            carried = dot(q, high) + dot(q, low)
            out_ref[rows, lanes] = dot(weights, v) + jnp.exp(c_column - base) * carried
            if b + 1 < TOKENS_HERE // BLOCK:
                last = c_here[:, -1:]
                decayed = k.T.astype(F32) * jnp.exp(last - c_here)
                high, low = split(decayed)
                state = jnp.exp(last - base) * state + dot(high, v) + dot(low, v)
                base = last


def inside(q, k, v, fading, pace, even, odd, first, heads, with_factor):
    at = first // GROUP
    wide = pl.BlockSpec((TOKENS_HERE, GROUP * HEAD_DIM), lambda g: (0, at + g))
    out_specs = [pl.BlockSpec((TOKENS_HERE, GROUP * HEAD_DIM), lambda g: (0, g))]
    out_shape = [jax.ShapeDtypeStruct((TOKENS_HERE, heads * HEAD_DIM), F32)]
    if with_factor:
        out_specs.append(pl.BlockSpec((TOKENS_HERE, 128), lambda g: (0, 0)))
        out_shape.append(jax.ShapeDtypeStruct((TOKENS_HERE, 128), F32))
    return pl.pallas_call(
        functools.partial(inside_kernel, first),
        grid=(heads // GROUP,),
        in_specs=[
            wide,
            wide,
            wide,
            pl.BlockSpec((HEADS_HERE, TOKENS_HERE), lambda g: (0, 0)),
            pl.BlockSpec((1, HEADS_HERE), lambda g: (0, 0)),
            pl.BlockSpec(even.shape, lambda g: (0, 0)),
            pl.BlockSpec(odd.shape, lambda g: (0, 0)),
        ],
        out_specs=out_specs,
        out_shape=out_shape,
        scratch_shapes=[
            pltpu.VMEM((HEADS_HERE, TOKENS_HERE), F32),
            pltpu.VMEM((TOKENS_HERE, 128), F32),
        ],
        compiler_params=pltpu.CompilerParams(vmem_limit_bytes=24 << 20),
        cost_estimate=pl.CostEstimate(
            flops=1_000_000_000, bytes_accessed=6 << 20, transcendentals=1 << 20
        ),
        name="inside",
    )(q, k, v, fading, pace, even, odd)


def outside_kernel(
    q_ref, low_ref, high_ref, own_ref, other_ref, factor_ref, out_ref, squares_ref, sum_ref
):
    g = pl.program_id(0)
    mine = lax.axis_index(CORE)

    @pl.when(g == 0)
    def _():
        sum_ref[...] = jnp.zeros_like(sum_ref)

    columns = pltpu.roll(factor_ref[...], lax.rem(128 - g * GROUP, 128), axis=1)
    own, other = own_ref[...], other_ref[...]
    even = jnp.where(mine == 0, own, other).reshape(16, 2, 8, 128)
    odd = jnp.where(mine == 0, other, own).reshape(16, 2, 8, 128)
    states = shuffle([even[:, 0], odd[:, 0], even[:, 1], odd[:, 1]])
    total = sum_ref[...]
    for i in range(GROUP):
        lanes = slice(i * HEAD_DIM, (i + 1) * HEAD_DIM)
        high, low = split(states[i].reshape(HEAD_DIM, HEAD_DIM))
        q = q_ref[:, lanes]
        carried = dot(jnp.concatenate([q, q], axis=1), jnp.concatenate([high, low], axis=0))
        before = jnp.where(g < GROUPS // 2, low_ref[:, lanes], high_ref[:, lanes])
        out = before + columns[:, i : i + 1] * carried
        out_ref[:, lanes] = out
        total = total + out * out
    sum_ref[...] = total

    @pl.when(g == GROUPS - 1)
    def _():
        squares_ref[...] = jnp.sum(total.T, axis=0, keepdims=True)


def outside(q, before_low, before_high, own, other, factor):
    width = GROUP * HEAD_DIM
    half = GROUPS // 2
    wide = pl.BlockSpec((TOKENS_HERE, width), lambda g: (0, g))
    pieces = pl.BlockSpec((CHIP_COUNT, 8, 128), lambda g: (0, g, 0))
    return pl.pallas_call(
        outside_kernel,
        grid=(GROUPS,),
        in_specs=[
            wide,
            pl.BlockSpec((TOKENS_HERE, width), lambda g: (0, jnp.minimum(g, half - 1))),
            pl.BlockSpec((TOKENS_HERE, width), lambda g: (0, jnp.maximum(g - half, 0))),
            pieces,
            pieces,
            pl.BlockSpec((TOKENS_HERE, 128), lambda g: (0, 0)),
        ],
        out_specs=[wide, pl.BlockSpec((1, TOKENS_HERE), lambda g: (0, 0))],
        out_shape=[
            jax.ShapeDtypeStruct((TOKENS_HERE, HEADS_HERE * HEAD_DIM), F32),
            jax.ShapeDtypeStruct((1, TOKENS_HERE), F32),
        ],
        scratch_shapes=[pltpu.VMEM((TOKENS_HERE, 128), F32)],
        compiler_params=pltpu.CompilerParams(vmem_limit_bytes=24 << 20),
        cost_estimate=pl.CostEstimate(
            flops=600_000_000, bytes_accessed=11 << 20, transcendentals=0
        ),
        name="outside",
    )(q, before_low, before_high, own, other, factor)


def norm_kernel(out_ref, *refs):
    *square_refs, gain_ref, result_ref = refs
    rows = out_ref.shape[0]
    total = sum(ref[...] for ref in square_refs)
    scale = lax.rsqrt(total / D + 1e-06)
    column = jnp.broadcast_to(scale, (128, rows)).T
    for h in range(HEADS_HERE):
        lanes = slice(h * HEAD_DIM, (h + 1) * HEAD_DIM)
        result_ref[:, lanes] = (out_ref[:, lanes] * column * gain_ref[:, lanes]).astype(BF16)


def normed(out, squares, gain):
    rows = 128
    width = HEADS_HERE * HEAD_DIM
    return pl.pallas_call(
        norm_kernel,
        grid=(TOKENS_HERE // rows,),
        in_specs=[
            pl.BlockSpec((rows, width), lambda t: (t, 0)),
            *(pl.BlockSpec((1, rows), lambda t: (0, t)) for _ in squares),
            pl.BlockSpec((1, width), lambda t: (0, 0)),
        ],
        out_specs=pl.BlockSpec((rows, width), lambda t: (t, 0)),
        out_shape=jax.ShapeDtypeStruct((TOKENS_HERE, width), BF16),
        compiler_params=pltpu.CompilerParams(vmem_limit_bytes=24 << 20),
        cost_estimate=pl.CostEstimate(flops=1 << 21, bytes_accessed=6 << 20, transcendentals=512),
        name="normed",
    )(out, *squares, gain)


def turned(value, by):
    count = lax.axis_size("tp")
    return lax.ppermute(value, "tp", [((i + by) % count, i) for i in range(count)])


def layer(q, k, v, pace, fading, gain):
    q, k, v, fading, pace = (
        pltpu.with_memory_space_constraint(part, pltpu.HBM)
        for part in (q, k, v, fading.T, pace.reshape(1, HEADS_HERE))
    )
    keep, send = local_states(k, v, fading, pace)
    swap = [(0, 1), (1, 0)]
    received = lax.ppermute(send, CORE, swap)
    chip, kept = chip_states(keep, received)
    partner = lax.ppermute(kept, CORE, swap)
    gathered = lax.all_to_all(chip.reshape(CHIP_COUNT, PIECE + 1, 1, 128), CHIPS, 0, 0, tiled=True)
    half = HEADS_HERE // 2
    arguments = (q, k, v, fading, pace, partner, received)
    before_low, factor = inside(*arguments, 0, half, True)
    before_low = pltpu.with_memory_space_constraint(before_low, pltpu.HBM)
    prior, final = scan_chips(gathered.reshape(CHIP_COUNT * (PIECE + 1), 128))
    own = lax.all_to_all(prior.reshape(CHIP_COUNT, PIECE, 128), CHIPS, 0, 0, tiled=True)
    (before_high,) = inside(*arguments, half, half, False)
    other = lax.ppermute(own, CORE, swap)
    out, squares = outside(q, before_low, before_high, own, other, factor)
    squares = [squares, *(turned(squares, by) for by in (1, 3, 2))]
    return normed(out, squares, gain.reshape(1, -1)), final


def solution(mesh):
    split_mesh = Mesh(
        mesh.devices.reshape(8, 4, 2, mesh.shape["tp"]), ("seq_0", "seq_1", "seq_2", "tp")
    )
    return jax.shard_map(
        layer,
        mesh=split_mesh,
        in_specs=(P(SEQ, "tp"), P(SEQ, "tp"), P(SEQ, "tp"), P("tp"), P(SEQ, "tp"), P("tp")),
        out_specs=(P(SEQ, "tp"), P("tp", SEQ)),
        check_vma=False,
    )
```

```python
import functools

import jax
import jax.numpy as jnp
from jax import lax
from jax.experimental import pallas as pl
from jax.experimental.pallas import tpu as pltpu
from jax.sharding import PartitionSpec as P

HEAD_DIM = 128
BLOCK = 256
D = 8192
SEQ = "seq"
SHARDS = 64
HEADS_HERE = 16
TOKENS_HERE = 512
GROUP = 4
GROUPS = HEADS_HERE // GROUP
CHIP_COUNT = 32
PIECE = 32
F32 = jnp.float32
BF16 = jnp.bfloat16


FORTH_REVERSED = True
BACK_REVERSED = True


def core_index():
    return lax.rem(lax.axis_index(SEQ), 2)


def groups(backwards):
    chips = range(CHIP_COUNT)[::-1] if backwards else range(CHIP_COUNT)
    return [[2 * chip + core for chip in chips] for core in range(2)]


def place(chip, backwards):
    return CHIP_COUNT - 1 - chip if backwards else chip


def dot(a, b, dims=((1,), (0,))):
    return lax.dot_general(a, b, (dims, ((), ())), preferred_element_type=F32)


def split(x):
    high = x.astype(BF16)
    return high, (x - high.astype(F32)).astype(BF16)


def log_decay(fading, pace):
    heads, tokens = fading.shape
    row = lax.broadcasted_iota(jnp.int32, (heads, heads), 0)
    col = lax.broadcasted_iota(jnp.int32, (heads, heads), 1)
    pace_column = jnp.sum(
        jnp.where(row == col, jnp.broadcast_to(pace, (heads, heads)), 0.0), axis=1, keepdims=True
    )
    c = fading - pace_column
    lane = lax.broadcasted_iota(jnp.int32, (heads, tokens), 1)
    shift = 1
    while shift < tokens:
        c = c + jnp.where(lane >= shift, pltpu.roll(c, shift, axis=1), 0.0)
        shift *= 2
    return c


def to_columns(rows):
    heads, tokens = rows.shape
    full = jnp.concatenate([rows, jnp.zeros((128 - heads, tokens), F32)], axis=0)
    return full.T


def total_row(c):
    heads = c.shape[0]
    last = jnp.broadcast_to(c[:, -1:], (heads, 128))
    row = lax.broadcasted_iota(jnp.int32, (heads, 128), 0)
    lane = lax.broadcasted_iota(jnp.int32, (heads, 128), 1)
    return jnp.sum(jnp.where(row == lane, last, 0.0), axis=0, keepdims=True)


def piece_column(row):
    r = lax.broadcasted_iota(jnp.int32, (PIECE, 128), 0)
    lane = lax.broadcasted_iota(jnp.int32, (PIECE, 128), 1)
    picked = jnp.where(lane == r // 2, jnp.broadcast_to(row, (PIECE, 128)), 0.0)
    return jnp.broadcast_to(jnp.sum(picked, axis=1, keepdims=True), (PIECE, 128))


def shuffle(x):
    sub = lax.broadcasted_iota(jnp.int32, x[0].shape, 1)
    for step in (1, 2):
        upper = ((sub // 2) & step) != 0
        y = list(x)
        for a in range(4):
            if a & step:
                continue
            b = a + step
            y[a] = jnp.where(upper, pltpu.roll(x[b], 2 * step, axis=1), x[a])
            y[b] = jnp.where(upper, x[b], pltpu.roll(x[a], 8 - 2 * step, axis=1))
        x = y
    return x


def state_kernel(
    k_hbm, v_hbm, fading_hbm, pace_hbm, keep_ref, send_ref, k_ref, v_ref, fading_ref, pace_ref, w_ref, sems
):
    mine = core_index()
    width = GROUP * HEAD_DIM
    small = [
        pltpu.make_async_copy(fading_hbm, fading_ref, sems.at[2 * GROUPS]),
        pltpu.make_async_copy(pace_hbm, pace_ref, sems.at[2 * GROUPS + 1]),
    ]
    for copy in small:
        copy.start()

    def copies(g):
        lanes = pl.ds(pl.multiple_of(g * width, width), width)
        return (
            pltpu.make_async_copy(k_hbm.at[:, lanes], k_ref.at[g], sems.at[g]),
            pltpu.make_async_copy(v_hbm.at[:, lanes], v_ref.at[g], sems.at[GROUPS + g]),
        )

    for g in range(GROUPS):
        for copy in copies(g):
            copy.start()
    for copy in small:
        copy.wait()
    c = log_decay(fading_ref[...], pace_ref[...])
    w_ref[...] = jnp.exp(c[:, -1:] - c)
    total = jnp.broadcast_to(total_row(c), (8, 128))
    keep_ref[pl.ds(CHIP_COUNT * PIECE, 8), :] = total
    send_ref[pl.ds(CHIP_COUNT * PIECE, 8), :] = total

    def group(g, carry):
        for copy in copies(g):
            copy.wait()
        states = []
        for i in range(GROUP):
            lanes = slice(i * HEAD_DIM, (i + 1) * HEAD_DIM)
            turned = k_ref[g, :, lanes].T.astype(F32)
            decayed = turned * w_ref[pl.ds(g * GROUP + i, 1), :]
            high, low = split(decayed)
            both = dot(jnp.concatenate([high, low], axis=0), v_ref[g, :, lanes])
            state = both[:HEAD_DIM] + both[HEAD_DIM:]
            states.append(state.reshape(16, 8, 128))
        units = shuffle(states)
        for b in range(2):
            even, odd = units[2 * b], units[2 * b + 1]
            kept = jnp.where(mine == 0, even, odd)
            sent = jnp.where(mine == 0, odd, even)
            for j in range(16):
                at = pl.ds(pl.multiple_of((2 * j + b) * PIECE + g * 8, 8), 8)
                keep_ref[at, :] = kept[j]
                send_ref[at, :] = sent[j]
        return carry

    lax.fori_loop(0, GROUPS, group, 0)


def local_states(k, v, fading, pace):
    rows = CHIP_COUNT * PIECE + 8
    return pl.pallas_call(
        state_kernel,
        in_specs=[pl.BlockSpec(memory_space=pl.ANY)] * 4,
        out_specs=[pl.BlockSpec(memory_space=pltpu.VMEM)] * 2,
        out_shape=[
            jax.ShapeDtypeStruct((rows, 128), F32),
            jax.ShapeDtypeStruct((rows, 128), F32),
        ],
        scratch_shapes=[
            pltpu.VMEM((GROUPS, TOKENS_HERE, GROUP * HEAD_DIM), BF16),
            pltpu.VMEM((GROUPS, TOKENS_HERE, GROUP * HEAD_DIM), BF16),
            pltpu.VMEM((HEADS_HERE, TOKENS_HERE), F32),
            pltpu.VMEM((1, HEADS_HERE), F32),
            pltpu.VMEM((HEADS_HERE, TOKENS_HERE), F32),
            pltpu.SemaphoreType.DMA((2 * GROUPS + 2,)),
        ],
        compiler_params=pltpu.CompilerParams(vmem_limit_bytes=24 << 20),
        cost_estimate=pl.CostEstimate(flops=600_000_000, bytes_accessed=6 << 20, transcendentals=8192),
        name="local_states",
    )(k, v, fading, pace)


def chip_kernel(own_ref, other_ref, out_ref, _):
    mine = core_index()
    tail = pl.ds(CHIP_COUNT * PIECE, 1)
    own_total, other_total = own_ref[tail, :], other_ref[tail, :]
    later = piece_column(jnp.exp(jnp.where(mine == 0, other_total, own_total)))
    own_factor = jnp.where(mine == 0, later, 1.0)
    other_factor = jnp.where(mine == 0, 1.0, later)
    total = own_total + other_total
    for p in range(CHIP_COUNT):
        at = pl.ds(p * PIECE, PIECE)
        to = place(p, FORTH_REVERSED) * (PIECE + 1)
        out_ref[pl.ds(to, PIECE), :] = (
            own_factor * own_ref[at, :] + other_factor * other_ref[at, :]
        )
        out_ref[pl.ds(to + PIECE, 1), :] = total


def chip_states(own, other):
    return pl.pallas_call(
        chip_kernel,
        in_specs=[pl.BlockSpec(memory_space=pltpu.VMEM)] * 2,
        out_specs=[pl.BlockSpec(memory_space=pltpu.VMEM)] * 2,
        out_shape=[
            jax.ShapeDtypeStruct((CHIP_COUNT * (PIECE + 1), 128), F32),
            jax.ShapeDtypeStruct(own.shape, F32),
        ],
        input_output_aliases={0: 1},
        compiler_params=pltpu.CompilerParams(vmem_limit_bytes=8 << 20),
        cost_estimate=pl.CostEstimate(flops=1 << 19, bytes_accessed=3 << 19, transcendentals=128),
        name="chip_states",
    )(own, other)


def scan_kernel(in_ref, out_ref, final_ref, last_ref):
    state = jnp.zeros((PIECE, 128), F32)
    for p in range(CHIP_COUNT):
        out_ref[pl.ds(place(p, BACK_REVERSED) * PIECE, PIECE), :] = state
        at = place(p, FORTH_REVERSED) * (PIECE + 1)
        factor = piece_column(jnp.exp(in_ref[pl.ds(at + PIECE, 1), :]))
        state = factor * state + in_ref[pl.ds(at, PIECE), :]
    last_ref[...] = state
    for i in range(2):
        final_ref[:, i * 128 : (i + 1) * 128] = last_ref[pl.ds(i, HEADS_HERE, stride=2), :]


def scan_chips(pieces):
    return pl.pallas_call(
        scan_kernel,
        out_shape=[
            jax.ShapeDtypeStruct((CHIP_COUNT * PIECE, 128), F32),
            jax.ShapeDtypeStruct((HEADS_HERE, 2 * HEAD_DIM), F32),
        ],
        scratch_shapes=[pltpu.VMEM((PIECE, 128), F32)],
        compiler_params=pltpu.CompilerParams(vmem_limit_bytes=8 << 20),
        cost_estimate=pl.CostEstimate(flops=1 << 19, bytes_accessed=1 << 20, transcendentals=4096),
        name="scan_chips",
    )(pieces)


def inside_kernel(
    first, q_ref, k_ref, v_ref, fading_ref, pace_ref, even_ref, odd_ref, out_ref, *more
):
    *factor_ref, c_ref, column_ref = more
    g = pl.program_id(0)
    h0 = first + g * GROUP
    second = core_index() == 1

    @pl.when(g == 0)
    def _():
        c = log_decay(fading_ref[...], pace_ref[...])
        c_ref[...] = c
        column_ref[...] = to_columns(c)
        if factor_ref:
            partner = jnp.where(second, odd_ref[pl.ds(CHIP_COUNT * PIECE, 1), :], 0.0)
            factor_ref[0][...] = jnp.exp(column_ref[...] + partner)

    columns = pltpu.roll(column_ref[...], lax.rem(128 - h0, 128), axis=1)
    starts = shuffle(
        [
            jnp.stack(
                [
                    jnp.where(second, ref[pl.ds(pl.multiple_of((2 * j + b) * PIECE + 2 * h0, 8), 8), :], 0.0)
                    for j in range(16)
                ]
            )
            for b in range(2)
            for ref in (even_ref, odd_ref)
        ]
    )
    row = lax.broadcasted_iota(jnp.int32, (BLOCK, BLOCK), 0)
    col = lax.broadcasted_iota(jnp.int32, (BLOCK, BLOCK), 1)
    for i in range(GROUP):
        lanes = slice(i * HEAD_DIM, (i + 1) * HEAD_DIM)
        c_row = c_ref[pl.ds(h0 + i, 1), :]
        state = starts[i].reshape(HEAD_DIM, HEAD_DIM)
        base = jnp.zeros((1, 1), F32)
        for b in range(TOKENS_HERE // BLOCK):
            rows = slice(b * BLOCK, (b + 1) * BLOCK)
            q, k, v = q_ref[rows, lanes], k_ref[rows, lanes], v_ref[rows, lanes]
            c_here = c_row[:, rows]
            c_column = columns[rows, i : i + 1]
            diff = c_column - c_here
            factor = jnp.where(row >= col, jnp.exp(jnp.minimum(diff, 0.0)), 0.0)
            weights = (dot(q, k, ((1,), (1,))) * factor).astype(BF16)
            high, low = split(state)
            carried = dot(q, high) + dot(q, low)
            out_ref[rows, lanes] = dot(weights, v) + jnp.exp(c_column - base) * carried
            if b + 1 < TOKENS_HERE // BLOCK:
                last = c_here[:, -1:]
                decayed = k.T.astype(F32) * jnp.exp(last - c_here)
                high, low = split(decayed)
                state = jnp.exp(last - base) * state + dot(high, v) + dot(low, v)
                base = last


def inside(q, k, v, fading, pace, even, odd, first, heads, with_factor):
    at = first // GROUP
    wide = pl.BlockSpec((TOKENS_HERE, GROUP * HEAD_DIM), lambda g: (0, at + g))
    out_specs = [pl.BlockSpec((TOKENS_HERE, GROUP * HEAD_DIM), lambda g: (0, g))]
    out_shape = [jax.ShapeDtypeStruct((TOKENS_HERE, heads * HEAD_DIM), F32)]
    if with_factor:
        out_specs.append(pl.BlockSpec((TOKENS_HERE, 128), lambda g: (0, 0)))
        out_shape.append(jax.ShapeDtypeStruct((TOKENS_HERE, 128), F32))
    return pl.pallas_call(
        functools.partial(inside_kernel, first),
        grid=(heads // GROUP,),
        in_specs=[
            wide,
            wide,
            wide,
            pl.BlockSpec((HEADS_HERE, TOKENS_HERE), lambda g: (0, 0)),
            pl.BlockSpec((1, HEADS_HERE), lambda g: (0, 0)),
            pl.BlockSpec(even.shape, lambda g: (0, 0)),
            pl.BlockSpec(odd.shape, lambda g: (0, 0)),
        ],
        out_specs=out_specs,
        out_shape=out_shape,
        scratch_shapes=[
            pltpu.VMEM((HEADS_HERE, TOKENS_HERE), F32),
            pltpu.VMEM((TOKENS_HERE, 128), F32),
        ],
        compiler_params=pltpu.CompilerParams(vmem_limit_bytes=24 << 20),
        cost_estimate=pl.CostEstimate(
            flops=1_000_000_000, bytes_accessed=6 << 20, transcendentals=1 << 20
        ),
        name="inside",
    )(q, k, v, fading, pace, even, odd)


def outside_kernel(
    q_hbm, low_hbm, own_hbm, high_ref, other_ref, factor_ref, out_ref, squares_ref, q_ref, low_ref, own_ref, sum_ref, sems
):
    mine = core_index()
    width = GROUP * HEAD_DIM
    half = GROUPS // 2
    own_copy = pltpu.make_async_copy(own_hbm, own_ref, sems.at[2 * GROUPS])
    own_copy.start()

    def copies(g, low):
        lanes = pl.ds(pl.multiple_of(g * width, width), width)
        found = [pltpu.make_async_copy(q_hbm.at[:, lanes], q_ref.at[g], sems.at[g])]
        if low:
            found.append(pltpu.make_async_copy(low_hbm.at[:, lanes], low_ref.at[g], sems.at[GROUPS + g]))
        return found

    for g in range(GROUPS):
        for copy in copies(g, g < half):
            copy.start()
    own_copy.wait()

    def group(g, low):
        for copy in copies(g, low):
            copy.wait()
        columns = pltpu.roll(factor_ref[...], lax.rem(128 - g * GROUP, 128), axis=1)
        rows = pl.ds(pl.multiple_of(g * 8, 8), 8)
        own, other = (
            jnp.stack([ref[place(p, BACK_REVERSED), rows, :] for p in range(CHIP_COUNT)])
            for ref in (own_ref, other_ref)
        )
        even = jnp.where(mine == 0, own, other).reshape(16, 2, 8, 128)
        odd = jnp.where(mine == 0, other, own).reshape(16, 2, 8, 128)
        states = shuffle([even[:, 0], odd[:, 0], even[:, 1], odd[:, 1]])
        start = g * width if low else (g - half) * width
        total = None
        for i in range(GROUP):
            lanes = slice(i * HEAD_DIM, (i + 1) * HEAD_DIM)
            high, low_part = split(states[i].reshape(HEAD_DIM, HEAD_DIM))
            q = q_ref[g, :, lanes]
            carried = dot(jnp.concatenate([q, q], axis=1), jnp.concatenate([high, low_part], axis=0))
            if low:
                before = low_ref[g, :, lanes]
            else:
                before = high_ref[:, pl.ds(pl.multiple_of(start + i * HEAD_DIM, HEAD_DIM), HEAD_DIM)]
            out = before + columns[:, i : i + 1] * carried
            out_ref[:, pl.ds(pl.multiple_of(g * width + i * HEAD_DIM, HEAD_DIM), HEAD_DIM)] = out
            total = out * out if total is None else total + out * out
        return total

    sum_ref[...] = jnp.zeros_like(sum_ref)

    def low_group(g, carry):
        sum_ref[...] += group(g, True)
        return carry

    def high_group(g, carry):
        sum_ref[...] += group(g, False)
        return carry

    lax.fori_loop(0, half, low_group, 0)
    lax.fori_loop(half, GROUPS, high_group, 0)
    squares_ref[...] = jnp.sum(sum_ref[...].T, axis=0, keepdims=True)


def outside(q, before_low, before_high, own, other, factor):
    width = GROUP * HEAD_DIM
    half = GROUPS // 2
    here = pl.BlockSpec(memory_space=pltpu.VMEM)
    return pl.pallas_call(
        outside_kernel,
        in_specs=[pl.BlockSpec(memory_space=pl.ANY)] * 3 + [here] * 3,
        out_specs=[here, here],
        out_shape=[
            jax.ShapeDtypeStruct((TOKENS_HERE, HEADS_HERE * HEAD_DIM), F32),
            jax.ShapeDtypeStruct((1, TOKENS_HERE), F32),
        ],
        scratch_shapes=[
            pltpu.VMEM((GROUPS, TOKENS_HERE, width), BF16),
            pltpu.VMEM((half, TOKENS_HERE, width), F32),
            pltpu.VMEM(own.shape, F32),
            pltpu.VMEM((TOKENS_HERE, 128), F32),
            pltpu.SemaphoreType.DMA((2 * GROUPS + 1,)),
        ],
        compiler_params=pltpu.CompilerParams(vmem_limit_bytes=24 << 20),
        cost_estimate=pl.CostEstimate(
            flops=600_000_000, bytes_accessed=11 << 20, transcendentals=0
        ),
        name="outside",
    )(q, before_low, own, before_high, other, factor)


NORM_ROWS = 64


def norm_kernel(out_ref, *refs):
    *square_refs, gain_ref, result_hbm, column_ref, result_ref, sems = refs
    total = sum(ref[...] for ref in square_refs)
    scale = lax.rsqrt(total / D + 1e-06)
    column_ref[...] = jnp.broadcast_to(scale, (128, TOKENS_HERE)).T
    steps = TOKENS_HERE // NORM_ROWS

    def write(t):
        rows = pl.ds(pl.multiple_of(t * NORM_ROWS, NORM_ROWS), NORM_ROWS)
        return pltpu.make_async_copy(result_ref.at[rows, :], result_hbm.at[rows, :], sems.at[t])

    def step(t, carry):
        rows = pl.ds(pl.multiple_of(t * NORM_ROWS, NORM_ROWS), NORM_ROWS)
        column = column_ref[rows, :]
        for h in range(HEADS_HERE):
            lanes = slice(h * HEAD_DIM, (h + 1) * HEAD_DIM)
            result_ref[rows, lanes] = (out_ref[rows, lanes] * column * gain_ref[:, lanes]).astype(BF16)
        write(t).start()
        return carry

    def finish(t, carry):
        write(t).wait()
        return carry

    lax.fori_loop(0, steps, step, 0)
    lax.fori_loop(0, steps, finish, 0)


def normed(out, squares, gain):
    width = HEADS_HERE * HEAD_DIM
    here = pl.BlockSpec(memory_space=pltpu.VMEM)
    return pl.pallas_call(
        norm_kernel,
        in_specs=[here] * (2 + len(squares)),
        out_specs=pl.BlockSpec(memory_space=pl.ANY),
        out_shape=jax.ShapeDtypeStruct((TOKENS_HERE, width), BF16),
        scratch_shapes=[
            pltpu.VMEM((TOKENS_HERE, 128), F32),
            pltpu.VMEM((TOKENS_HERE, width), BF16),
            pltpu.SemaphoreType.DMA((TOKENS_HERE // NORM_ROWS,)),
        ],
        compiler_params=pltpu.CompilerParams(vmem_limit_bytes=24 << 20),
        cost_estimate=pl.CostEstimate(flops=1 << 21, bytes_accessed=6 << 20, transcendentals=512),
        name="normed",
    )(out, *squares, gain)


def turned(value, by):
    count = lax.axis_size("tp")
    return lax.ppermute(value, "tp", [((i + by) % count, i) for i in range(count)])


def layer(q, k, v, pace, fading, gain):
    q, k, v, fading, pace = (
        pltpu.with_memory_space_constraint(part, pltpu.HBM)
        for part in (q, k, v, fading.T, pace.reshape(1, HEADS_HERE))
    )
    keep, send = local_states(k, v, fading, pace)
    swap = [(i, i ^ 1) for i in range(SHARDS)]
    received = lax.ppermute(send, SEQ, swap)
    chip, kept = chip_states(keep, received)
    partner = lax.ppermute(kept, SEQ, swap)
    gathered = lax.all_to_all(
        chip.reshape(CHIP_COUNT, PIECE + 1, 1, 128),
        SEQ,
        0,
        0,
        axis_index_groups=groups(FORTH_REVERSED),
        tiled=True,
    )
    half = HEADS_HERE // 2
    arguments = (q, k, v, fading, pace, partner, received)
    before_low, factor = inside(*arguments, 0, half, True)
    before_low = pltpu.with_memory_space_constraint(before_low, pltpu.HBM)
    prior, final = scan_chips(gathered.reshape(CHIP_COUNT * (PIECE + 1), 128))
    own = lax.all_to_all(
        prior.reshape(CHIP_COUNT, PIECE, 128),
        SEQ,
        0,
        0,
        axis_index_groups=groups(BACK_REVERSED),
        tiled=True,
    )
    (before_high,) = inside(*arguments, half, half, False)
    other = lax.ppermute(own, SEQ, swap)
    out, squares = outside(q, before_low, before_high, own, other, factor)
    squares = [squares, *(turned(squares, by) for by in (1, 3, 2))]
    return normed(out, squares, gain.reshape(1, -1)), final


def solution(mesh):
    return jax.shard_map(
        layer,
        mesh=mesh,
        in_specs=(P(SEQ, "tp"), P(SEQ, "tp"), P(SEQ, "tp"), P("tp"), P(SEQ, "tp"), P("tp")),
        out_specs=(P(SEQ, "tp"), P("tp", SEQ)),
        check_vma=False,
    )
```

```python
import functools

import jax
import jax.numpy as jnp
from jax import lax
from jax.experimental import pallas as pl
from jax.experimental.pallas import tpu as pltpu
from jax.sharding import PartitionSpec as P

HEAD_DIM = 128
BLOCK = 256
D = 8192
SEQ = "seq"
SHARDS = 64
HEADS_HERE = 16
TOKENS_HERE = 512
GROUP = 4
GROUPS = HEADS_HERE // GROUP
CHIP_COUNT = 32
PIECE = 32
F32 = jnp.float32
BF16 = jnp.bfloat16


FORTH_REVERSED = True
BACK_REVERSED = True


def core_index():
    return lax.rem(lax.axis_index(SEQ), 2)


def groups(backwards):
    chips = range(CHIP_COUNT)[::-1] if backwards else range(CHIP_COUNT)
    return [[2 * chip + core for chip in chips] for core in range(2)]


def place(chip, backwards):
    return CHIP_COUNT - 1 - chip if backwards else chip


def dot(a, b, dims=((1,), (0,))):
    return lax.dot_general(a, b, (dims, ((), ())), preferred_element_type=F32)


def split(x):
    high = x.astype(BF16)
    return high, (x - high.astype(F32)).astype(BF16)


def log_decay(fading, pace):
    heads, tokens = fading.shape
    row = lax.broadcasted_iota(jnp.int32, (heads, heads), 0)
    col = lax.broadcasted_iota(jnp.int32, (heads, heads), 1)
    pace_column = jnp.sum(
        jnp.where(row == col, jnp.broadcast_to(pace, (heads, heads)), 0.0), axis=1, keepdims=True
    )
    c = fading - pace_column
    lane = lax.broadcasted_iota(jnp.int32, (heads, tokens), 1)
    shift = 1
    while shift < tokens:
        c = c + jnp.where(lane >= shift, pltpu.roll(c, shift, axis=1), 0.0)
        shift *= 2
    return c


def to_columns(rows):
    heads, tokens = rows.shape
    full = jnp.concatenate([rows, jnp.zeros((128 - heads, tokens), F32)], axis=0)
    return full.T


def total_row(c):
    heads = c.shape[0]
    last = jnp.broadcast_to(c[:, -1:], (heads, 128))
    row = lax.broadcasted_iota(jnp.int32, (heads, 128), 0)
    lane = lax.broadcasted_iota(jnp.int32, (heads, 128), 1)
    return jnp.sum(jnp.where(row == lane, last, 0.0), axis=0, keepdims=True)


def piece_column(row):
    r = lax.broadcasted_iota(jnp.int32, (PIECE, 128), 0)
    lane = lax.broadcasted_iota(jnp.int32, (PIECE, 128), 1)
    picked = jnp.where(lane == r // 2, jnp.broadcast_to(row, (PIECE, 128)), 0.0)
    return jnp.broadcast_to(jnp.sum(picked, axis=1, keepdims=True), (PIECE, 128))


def shuffle(x):
    sub = lax.broadcasted_iota(jnp.int32, x[0].shape, 1)
    for step in (1, 2):
        upper = ((sub // 2) & step) != 0
        y = list(x)
        for a in range(4):
            if a & step:
                continue
            b = a + step
            y[a] = jnp.where(upper, pltpu.roll(x[b], 2 * step, axis=1), x[a])
            y[b] = jnp.where(upper, x[b], pltpu.roll(x[a], 8 - 2 * step, axis=1))
        x = y
    return x


def state_kernel(
    k_hbm, v_hbm, fading_hbm, pace_hbm, keep_ref, send_ref, k_ref, v_ref, fading_ref, pace_ref, w_ref, sems
):
    mine = core_index()
    width = GROUP * HEAD_DIM
    small = [
        pltpu.make_async_copy(fading_hbm, fading_ref, sems.at[2 * GROUPS]),
        pltpu.make_async_copy(pace_hbm, pace_ref, sems.at[2 * GROUPS + 1]),
    ]
    for copy in small:
        copy.start()

    def copies(g):
        lanes = pl.ds(pl.multiple_of(g * width, width), width)
        return (
            pltpu.make_async_copy(k_hbm.at[:, lanes], k_ref.at[g], sems.at[g]),
            pltpu.make_async_copy(v_hbm.at[:, lanes], v_ref.at[g], sems.at[GROUPS + g]),
        )

    for g in range(GROUPS):
        for copy in copies(g):
            copy.start()
    for copy in small:
        copy.wait()
    c = log_decay(fading_ref[...], pace_ref[...])
    w_ref[...] = jnp.exp(c[:, -1:] - c)
    total = jnp.broadcast_to(total_row(c), (8, 128))
    keep_ref[pl.ds(CHIP_COUNT * PIECE, 8), :] = total
    send_ref[pl.ds(CHIP_COUNT * PIECE, 8), :] = total

    def group(g, carry):
        for copy in copies(g):
            copy.wait()
        states = []
        for i in range(GROUP):
            lanes = slice(i * HEAD_DIM, (i + 1) * HEAD_DIM)
            turned = k_ref[g, :, lanes].T.astype(F32)
            decayed = turned * w_ref[pl.ds(g * GROUP + i, 1), :]
            high, low = split(decayed)
            both = dot(jnp.concatenate([high, low], axis=0), v_ref[g, :, lanes])
            state = both[:HEAD_DIM] + both[HEAD_DIM:]
            states.append(state.reshape(16, 8, 128))
        units = shuffle(states)
        for b in range(2):
            even, odd = units[2 * b], units[2 * b + 1]
            kept = jnp.where(mine == 0, even, odd)
            sent = jnp.where(mine == 0, odd, even)
            for j in range(16):
                at = pl.ds(pl.multiple_of((2 * j + b) * PIECE + g * 8, 8), 8)
                keep_ref[at, :] = kept[j]
                send_ref[at, :] = sent[j]
        return carry

    lax.fori_loop(0, GROUPS, group, 0)


def local_states(k, v, fading, pace):
    rows = CHIP_COUNT * PIECE + 8
    return pl.pallas_call(
        state_kernel,
        in_specs=[pl.BlockSpec(memory_space=pl.ANY)] * 4,
        out_specs=[pl.BlockSpec(memory_space=pltpu.VMEM)] * 2,
        out_shape=[
            jax.ShapeDtypeStruct((rows, 128), F32),
            jax.ShapeDtypeStruct((rows, 128), F32),
        ],
        scratch_shapes=[
            pltpu.VMEM((GROUPS, TOKENS_HERE, GROUP * HEAD_DIM), BF16),
            pltpu.VMEM((GROUPS, TOKENS_HERE, GROUP * HEAD_DIM), BF16),
            pltpu.VMEM((HEADS_HERE, TOKENS_HERE), F32),
            pltpu.VMEM((1, HEADS_HERE), F32),
            pltpu.VMEM((HEADS_HERE, TOKENS_HERE), F32),
            pltpu.SemaphoreType.DMA((2 * GROUPS + 2,)),
        ],
        compiler_params=pltpu.CompilerParams(vmem_limit_bytes=24 << 20),
        cost_estimate=pl.CostEstimate(flops=600_000_000, bytes_accessed=6 << 20, transcendentals=8192),
        name="local_states",
    )(k, v, fading, pace)


def chip_kernel(own_ref, other_ref, out_ref, _):
    mine = core_index()
    tail = pl.ds(CHIP_COUNT * PIECE, 1)
    own_total, other_total = own_ref[tail, :], other_ref[tail, :]
    later = piece_column(jnp.exp(jnp.where(mine == 0, other_total, own_total)))
    own_factor = jnp.where(mine == 0, later, 1.0)
    other_factor = jnp.where(mine == 0, 1.0, later)
    total = own_total + other_total
    for p in range(CHIP_COUNT):
        at = pl.ds(p * PIECE, PIECE)
        to = place(p, FORTH_REVERSED) * (PIECE + 1)
        out_ref[pl.ds(to, PIECE), :] = (
            own_factor * own_ref[at, :] + other_factor * other_ref[at, :]
        )
        out_ref[pl.ds(to + PIECE, 1), :] = total


def chip_states(own, other):
    return pl.pallas_call(
        chip_kernel,
        in_specs=[pl.BlockSpec(memory_space=pltpu.VMEM)] * 2,
        out_specs=[pl.BlockSpec(memory_space=pltpu.VMEM)] * 2,
        out_shape=[
            jax.ShapeDtypeStruct((CHIP_COUNT * (PIECE + 1), 128), F32),
            jax.ShapeDtypeStruct(own.shape, F32),
        ],
        input_output_aliases={0: 1},
        compiler_params=pltpu.CompilerParams(vmem_limit_bytes=8 << 20),
        cost_estimate=pl.CostEstimate(flops=1 << 19, bytes_accessed=3 << 19, transcendentals=128),
        name="chip_states",
    )(own, other)


def scan_kernel(in_ref, out_ref, final_ref, last_ref):
    state = jnp.zeros((PIECE, 128), F32)
    for p in range(CHIP_COUNT):
        out_ref[pl.ds(place(p, BACK_REVERSED) * PIECE, PIECE), :] = state
        at = place(p, FORTH_REVERSED) * (PIECE + 1)
        factor = piece_column(jnp.exp(in_ref[pl.ds(at + PIECE, 1), :]))
        state = factor * state + in_ref[pl.ds(at, PIECE), :]
    last_ref[...] = state
    for i in range(2):
        final_ref[:, i * 128 : (i + 1) * 128] = last_ref[pl.ds(i, HEADS_HERE, stride=2), :]


def scan_chips(pieces):
    return pl.pallas_call(
        scan_kernel,
        out_shape=[
            jax.ShapeDtypeStruct((CHIP_COUNT * PIECE, 128), F32),
            jax.ShapeDtypeStruct((HEADS_HERE, 2 * HEAD_DIM), F32),
        ],
        scratch_shapes=[pltpu.VMEM((PIECE, 128), F32)],
        compiler_params=pltpu.CompilerParams(vmem_limit_bytes=8 << 20),
        cost_estimate=pl.CostEstimate(flops=1 << 19, bytes_accessed=1 << 20, transcendentals=4096),
        name="scan_chips",
    )(pieces)


def inside_kernel(
    first, q_ref, k_ref, v_ref, fading_ref, pace_ref, even_ref, odd_ref, out_ref, *more
):
    *factor_ref, c_ref, column_ref = more
    g = pl.program_id(0)
    h0 = first + g * GROUP
    second = core_index() == 1

    @pl.when(g == 0)
    def _():
        c = log_decay(fading_ref[...], pace_ref[...])
        c_ref[...] = c
        column_ref[...] = to_columns(c)
        if factor_ref:
            partner = jnp.where(second, odd_ref[pl.ds(CHIP_COUNT * PIECE, 1), :], 0.0)
            factor_ref[0][...] = jnp.exp(column_ref[...] + partner)

    columns = pltpu.roll(column_ref[...], lax.rem(128 - h0, 128), axis=1)
    starts = shuffle(
        [
            jnp.stack(
                [
                    jnp.where(second, ref[pl.ds(pl.multiple_of((2 * j + b) * PIECE + 2 * h0, 8), 8), :], 0.0)
                    for j in range(16)
                ]
            )
            for b in range(2)
            for ref in (even_ref, odd_ref)
        ]
    )
    row = lax.broadcasted_iota(jnp.int32, (BLOCK, BLOCK), 0)
    col = lax.broadcasted_iota(jnp.int32, (BLOCK, BLOCK), 1)
    for i in range(GROUP):
        lanes = slice(i * HEAD_DIM, (i + 1) * HEAD_DIM)
        c_row = c_ref[pl.ds(h0 + i, 1), :]
        state = starts[i].reshape(HEAD_DIM, HEAD_DIM)
        base = jnp.zeros((1, 1), F32)
        for b in range(TOKENS_HERE // BLOCK):
            rows = slice(b * BLOCK, (b + 1) * BLOCK)
            q, k, v = q_ref[rows, lanes], k_ref[rows, lanes], v_ref[rows, lanes]
            c_here = c_row[:, rows]
            c_column = columns[rows, i : i + 1]
            diff = c_column - c_here
            factor = jnp.where(row >= col, jnp.exp(jnp.minimum(diff, 0.0)), 0.0)
            weights = (dot(q, k, ((1,), (1,))) * factor).astype(BF16)
            high, low = split(state)
            carried = dot(q, high) + dot(q, low)
            out_ref[rows, lanes] = dot(weights, v) + jnp.exp(c_column - base) * carried
            if b + 1 < TOKENS_HERE // BLOCK:
                last = c_here[:, -1:]
                decayed = k.T.astype(F32) * jnp.exp(last - c_here)
                high, low = split(decayed)
                state = jnp.exp(last - base) * state + dot(high, v) + dot(low, v)
                base = last


def inside(q, k, v, fading, pace, even, odd, first, heads, with_factor):
    at = first // GROUP
    wide = pl.BlockSpec((TOKENS_HERE, GROUP * HEAD_DIM), lambda g: (0, at + g))
    out_specs = [pl.BlockSpec((TOKENS_HERE, GROUP * HEAD_DIM), lambda g: (0, g))]
    out_shape = [jax.ShapeDtypeStruct((TOKENS_HERE, heads * HEAD_DIM), F32)]
    if with_factor:
        out_specs.append(pl.BlockSpec((TOKENS_HERE, 128), lambda g: (0, 0)))
        out_shape.append(jax.ShapeDtypeStruct((TOKENS_HERE, 128), F32))
    return pl.pallas_call(
        functools.partial(inside_kernel, first),
        grid=(heads // GROUP,),
        in_specs=[
            wide,
            wide,
            wide,
            pl.BlockSpec((HEADS_HERE, TOKENS_HERE), lambda g: (0, 0)),
            pl.BlockSpec((1, HEADS_HERE), lambda g: (0, 0)),
            pl.BlockSpec(even.shape, lambda g: (0, 0)),
            pl.BlockSpec(odd.shape, lambda g: (0, 0)),
        ],
        out_specs=out_specs,
        out_shape=out_shape,
        scratch_shapes=[
            pltpu.VMEM((HEADS_HERE, TOKENS_HERE), F32),
            pltpu.VMEM((TOKENS_HERE, 128), F32),
        ],
        compiler_params=pltpu.CompilerParams(vmem_limit_bytes=24 << 20),
        cost_estimate=pl.CostEstimate(
            flops=1_000_000_000, bytes_accessed=6 << 20, transcendentals=1 << 20
        ),
        name="inside",
    )(q, k, v, fading, pace, even, odd)


def fetch_kernel(*refs):
    count = len(refs) // 2
    *refs, sems = refs
    copies = [
        pltpu.make_async_copy(source, target, sems.at[n])
        for n, (source, target) in enumerate(zip(refs[:count], refs[count:]))
    ]
    for copy in copies:
        copy.start()
    for copy in copies:
        copy.wait()


def fetched(*arrays):
    return pl.pallas_call(
        fetch_kernel,
        in_specs=[pl.BlockSpec(memory_space=pl.ANY)] * len(arrays),
        out_specs=[pl.BlockSpec(memory_space=pltpu.VMEM)] * len(arrays),
        out_shape=[jax.ShapeDtypeStruct(array.shape, array.dtype) for array in arrays],
        scratch_shapes=[pltpu.SemaphoreType.DMA((len(arrays),))],
        compiler_params=pltpu.CompilerParams(vmem_limit_bytes=8 << 20),
        cost_estimate=pl.CostEstimate(flops=0, bytes_accessed=9 << 20, transcendentals=0),
        name="fetched",
    )(*arrays)


def outside_kernel(
    q_ref, low_ref, own_ref, high_ref, other_ref, factor_ref, out_ref, squares_ref, sum_ref
):
    mine = core_index()
    width = GROUP * HEAD_DIM
    half = GROUPS // 2

    def group(g, low):
        columns = pltpu.roll(factor_ref[...], lax.rem(128 - g * GROUP, 128), axis=1)
        rows = pl.ds(pl.multiple_of(g * 8, 8), 8)
        own, other = (
            jnp.stack([ref[place(p, BACK_REVERSED), rows, :] for p in range(CHIP_COUNT)])
            for ref in (own_ref, other_ref)
        )
        even = jnp.where(mine == 0, own, other).reshape(16, 2, 8, 128)
        odd = jnp.where(mine == 0, other, own).reshape(16, 2, 8, 128)
        states = shuffle([even[:, 0], odd[:, 0], even[:, 1], odd[:, 1]])
        before_ref, start = (low_ref, 0) if low else (high_ref, half)
        total = None
        for i in range(GROUP):
            high, low_part = split(states[i].reshape(HEAD_DIM, HEAD_DIM))
            here = pl.ds(pl.multiple_of(g * width + i * HEAD_DIM, HEAD_DIM), HEAD_DIM)
            there = pl.ds(pl.multiple_of((g - start) * width + i * HEAD_DIM, HEAD_DIM), HEAD_DIM)
            q = q_ref[:, here]
            carried = dot(jnp.concatenate([q, q], axis=1), jnp.concatenate([high, low_part], axis=0))
            out = before_ref[:, there] + columns[:, i : i + 1] * carried
            out_ref[:, here] = out
            total = out * out if total is None else total + out * out
        return total

    sum_ref[...] = jnp.zeros_like(sum_ref)

    def low_group(g, carry):
        sum_ref[...] += group(g, True)
        return carry

    def high_group(g, carry):
        sum_ref[...] += group(g, False)
        return carry

    lax.fori_loop(0, half, low_group, 0)
    lax.fori_loop(half, GROUPS, high_group, 0)
    squares_ref[...] = jnp.sum(sum_ref[...].T, axis=0, keepdims=True)


def outside(q, before_low, own, before_high, other, factor):
    here = pl.BlockSpec(memory_space=pltpu.VMEM)
    return pl.pallas_call(
        outside_kernel,
        in_specs=[here] * 6,
        out_specs=[here, here],
        out_shape=[
            jax.ShapeDtypeStruct((TOKENS_HERE, HEADS_HERE * HEAD_DIM), F32),
            jax.ShapeDtypeStruct((1, TOKENS_HERE), F32),
        ],
        scratch_shapes=[pltpu.VMEM((TOKENS_HERE, 128), F32)],
        compiler_params=pltpu.CompilerParams(vmem_limit_bytes=24 << 20),
        cost_estimate=pl.CostEstimate(
            flops=600_000_000, bytes_accessed=11 << 20, transcendentals=0
        ),
        name="outside",
    )(q, before_low, own, before_high, other, factor)


NORM_ROWS = 64


def norm_kernel(out_ref, *refs):
    *square_refs, gain_ref, result_hbm, column_ref, result_ref, sems = refs
    total = sum(ref[...] for ref in square_refs)
    scale = lax.rsqrt(total / D + 1e-06)
    column_ref[...] = jnp.broadcast_to(scale, (128, TOKENS_HERE)).T
    steps = TOKENS_HERE // NORM_ROWS

    def write(t):
        rows = pl.ds(pl.multiple_of(t * NORM_ROWS, NORM_ROWS), NORM_ROWS)
        return pltpu.make_async_copy(result_ref.at[rows, :], result_hbm.at[rows, :], sems.at[t])

    def step(t, carry):
        rows = pl.ds(pl.multiple_of(t * NORM_ROWS, NORM_ROWS), NORM_ROWS)
        column = column_ref[rows, :]
        for h in range(HEADS_HERE):
            lanes = slice(h * HEAD_DIM, (h + 1) * HEAD_DIM)
            result_ref[rows, lanes] = (out_ref[rows, lanes] * column * gain_ref[:, lanes]).astype(BF16)
        write(t).start()
        return carry

    def finish(t, carry):
        write(t).wait()
        return carry

    lax.fori_loop(0, steps, step, 0)
    lax.fori_loop(0, steps, finish, 0)


def normed(out, squares, gain):
    width = HEADS_HERE * HEAD_DIM
    here = pl.BlockSpec(memory_space=pltpu.VMEM)
    return pl.pallas_call(
        norm_kernel,
        in_specs=[here] * (2 + len(squares)),
        out_specs=pl.BlockSpec(memory_space=pl.ANY),
        out_shape=jax.ShapeDtypeStruct((TOKENS_HERE, width), BF16),
        scratch_shapes=[
            pltpu.VMEM((TOKENS_HERE, 128), F32),
            pltpu.VMEM((TOKENS_HERE, width), BF16),
            pltpu.SemaphoreType.DMA((TOKENS_HERE // NORM_ROWS,)),
        ],
        compiler_params=pltpu.CompilerParams(vmem_limit_bytes=24 << 20),
        cost_estimate=pl.CostEstimate(flops=1 << 21, bytes_accessed=6 << 20, transcendentals=512),
        name="normed",
    )(out, *squares, gain)


def turned(value, by):
    count = lax.axis_size("tp")
    return lax.ppermute(value, "tp", [((i + by) % count, i) for i in range(count)])


def layer(q, k, v, pace, fading, gain):
    q, k, v, fading, pace = (
        pltpu.with_memory_space_constraint(part, pltpu.HBM)
        for part in (q, k, v, fading.T, pace.reshape(1, HEADS_HERE))
    )
    keep, send = local_states(k, v, fading, pace)
    swap = [(i, i ^ 1) for i in range(SHARDS)]
    received = lax.ppermute(send, SEQ, swap)
    chip, kept = chip_states(keep, received)
    partner = lax.ppermute(kept, SEQ, swap)
    gathered = lax.all_to_all(
        chip.reshape(CHIP_COUNT, PIECE + 1, 1, 128),
        SEQ,
        0,
        0,
        axis_index_groups=groups(FORTH_REVERSED),
        tiled=True,
    )
    half = HEADS_HERE // 2
    arguments = (q, k, v, fading, pace, partner, received)
    before_low, factor = inside(*arguments, 0, half, True)
    before_low = pltpu.with_memory_space_constraint(before_low, pltpu.HBM)
    prior, final = scan_chips(gathered.reshape(CHIP_COUNT * (PIECE + 1), 128))
    own = lax.all_to_all(
        prior.reshape(CHIP_COUNT, PIECE, 128),
        SEQ,
        0,
        0,
        axis_index_groups=groups(BACK_REVERSED),
        tiled=True,
    )
    (before_high,) = inside(*arguments, half, half, False)
    other = lax.ppermute(own, SEQ, swap)
    near = fetched(q, before_low, own)
    out, squares = outside(*near, before_high, other, factor)
    squares = [squares, *(turned(squares, by) for by in (1, 3, 2))]
    return normed(out, squares, gain.reshape(1, -1)), final


def solution(mesh):
    return jax.shard_map(
        layer,
        mesh=mesh,
        in_specs=(P(SEQ, "tp"), P(SEQ, "tp"), P(SEQ, "tp"), P("tp"), P(SEQ, "tp"), P("tp")),
        out_specs=(P(SEQ, "tp"), P("tp", SEQ)),
        check_vma=False,
    )
```

```python
import functools

import jax
import jax.numpy as jnp
from jax import lax
from jax.experimental import pallas as pl
from jax.experimental.pallas import tpu as pltpu
from jax.sharding import PartitionSpec as P

HEAD_DIM = 128
BLOCK = 256
D = 8192
SEQ = "seq"
SHARDS = 64
HEADS_HERE = 16
TOKENS_HERE = 512
GROUP = 4
GROUPS = HEADS_HERE // GROUP
CHIP_COUNT = 32
PIECE = 32
F32 = jnp.float32
BF16 = jnp.bfloat16


FORTH_REVERSED = True
BACK_REVERSED = True


def core_index():
    return lax.rem(lax.axis_index(SEQ), 2)


def groups(backwards):
    chips = range(CHIP_COUNT)[::-1] if backwards else range(CHIP_COUNT)
    return [[2 * chip + core for chip in chips] for core in range(2)]


def place(chip, backwards):
    return CHIP_COUNT - 1 - chip if backwards else chip


def dot(a, b, dims=((1,), (0,))):
    return lax.dot_general(a, b, (dims, ((), ())), preferred_element_type=F32)


def split(x):
    high = x.astype(BF16)
    return high, (x - high.astype(F32)).astype(BF16)


def log_decay(fading, pace):
    heads, tokens = fading.shape
    row = lax.broadcasted_iota(jnp.int32, (heads, heads), 0)
    col = lax.broadcasted_iota(jnp.int32, (heads, heads), 1)
    pace_column = jnp.sum(
        jnp.where(row == col, jnp.broadcast_to(pace, (heads, heads)), 0.0), axis=1, keepdims=True
    )
    c = fading - pace_column
    lane = lax.broadcasted_iota(jnp.int32, (heads, tokens), 1)
    shift = 1
    while shift < tokens:
        c = c + jnp.where(lane >= shift, pltpu.roll(c, shift, axis=1), 0.0)
        shift *= 2
    return c


def to_columns(rows):
    heads, tokens = rows.shape
    full = jnp.concatenate([rows, jnp.zeros((128 - heads, tokens), F32)], axis=0)
    return full.T


def total_row(c):
    heads = c.shape[0]
    last = jnp.broadcast_to(c[:, -1:], (heads, 128))
    row = lax.broadcasted_iota(jnp.int32, (heads, 128), 0)
    lane = lax.broadcasted_iota(jnp.int32, (heads, 128), 1)
    return jnp.sum(jnp.where(row == lane, last, 0.0), axis=0, keepdims=True)


def piece_column(row):
    r = lax.broadcasted_iota(jnp.int32, (PIECE, 128), 0)
    lane = lax.broadcasted_iota(jnp.int32, (PIECE, 128), 1)
    picked = jnp.where(lane == r // 2, jnp.broadcast_to(row, (PIECE, 128)), 0.0)
    return jnp.broadcast_to(jnp.sum(picked, axis=1, keepdims=True), (PIECE, 128))


def shuffle(x):
    sub = lax.broadcasted_iota(jnp.int32, x[0].shape, 1)
    for step in (1, 2):
        upper = ((sub // 2) & step) != 0
        y = list(x)
        for a in range(4):
            if a & step:
                continue
            b = a + step
            y[a] = jnp.where(upper, pltpu.roll(x[b], 2 * step, axis=1), x[a])
            y[b] = jnp.where(upper, x[b], pltpu.roll(x[a], 8 - 2 * step, axis=1))
        x = y
    return x


def state_kernel(
    k_hbm, v_hbm, fading_hbm, pace_hbm, keep_ref, send_ref, k_ref, v_ref, fading_ref, pace_ref, w_ref, sems
):
    mine = core_index()
    width = GROUP * HEAD_DIM
    small = [
        pltpu.make_async_copy(fading_hbm, fading_ref, sems.at[2 * GROUPS]),
        pltpu.make_async_copy(pace_hbm, pace_ref, sems.at[2 * GROUPS + 1]),
    ]
    for copy in small:
        copy.start()

    def copies(g):
        lanes = pl.ds(pl.multiple_of(g * width, width), width)
        return (
            pltpu.make_async_copy(k_hbm.at[:, lanes], k_ref.at[g], sems.at[g]),
            pltpu.make_async_copy(v_hbm.at[:, lanes], v_ref.at[g], sems.at[GROUPS + g]),
        )

    for g in range(GROUPS):
        for copy in copies(g):
            copy.start()
    for copy in small:
        copy.wait()
    c = log_decay(fading_ref[...], pace_ref[...])
    w_ref[...] = jnp.exp(c[:, -1:] - c)
    total = jnp.broadcast_to(total_row(c), (8, 128))
    keep_ref[pl.ds(CHIP_COUNT * PIECE, 8), :] = total
    send_ref[pl.ds(CHIP_COUNT * PIECE, 8), :] = total

    def group(g, carry):
        for copy in copies(g):
            copy.wait()
        states = []
        for i in range(GROUP):
            lanes = slice(i * HEAD_DIM, (i + 1) * HEAD_DIM)
            turned = k_ref[g, :, lanes].T.astype(F32)
            decayed = turned * w_ref[pl.ds(g * GROUP + i, 1), :]
            high, low = split(decayed)
            both = dot(jnp.concatenate([high, low], axis=0), v_ref[g, :, lanes])
            state = both[:HEAD_DIM] + both[HEAD_DIM:]
            states.append(state.reshape(16, 8, 128))
        units = shuffle(states)
        for b in range(2):
            even, odd = units[2 * b], units[2 * b + 1]
            kept = jnp.where(mine == 0, even, odd)
            sent = jnp.where(mine == 0, odd, even)
            for j in range(16):
                at = pl.ds(pl.multiple_of((2 * j + b) * PIECE + g * 8, 8), 8)
                keep_ref[at, :] = kept[j]
                send_ref[at, :] = sent[j]
        return carry

    lax.fori_loop(0, GROUPS, group, 0)


def local_states(k, v, fading, pace):
    rows = CHIP_COUNT * PIECE + 8
    return pl.pallas_call(
        state_kernel,
        in_specs=[pl.BlockSpec(memory_space=pl.ANY)] * 4,
        out_specs=[pl.BlockSpec(memory_space=pltpu.VMEM)] * 2,
        out_shape=[
            jax.ShapeDtypeStruct((rows, 128), F32),
            jax.ShapeDtypeStruct((rows, 128), F32),
        ],
        scratch_shapes=[
            pltpu.VMEM((GROUPS, TOKENS_HERE, GROUP * HEAD_DIM), BF16),
            pltpu.VMEM((GROUPS, TOKENS_HERE, GROUP * HEAD_DIM), BF16),
            pltpu.VMEM((HEADS_HERE, TOKENS_HERE), F32),
            pltpu.VMEM((1, HEADS_HERE), F32),
            pltpu.VMEM((HEADS_HERE, TOKENS_HERE), F32),
            pltpu.SemaphoreType.DMA((2 * GROUPS + 2,)),
        ],
        compiler_params=pltpu.CompilerParams(vmem_limit_bytes=24 << 20),
        cost_estimate=pl.CostEstimate(flops=600_000_000, bytes_accessed=6 << 20, transcendentals=8192),
        name="local_states",
    )(k, v, fading, pace)


def chip_kernel(own_ref, other_ref, out_ref, _):
    mine = core_index()
    tail = pl.ds(CHIP_COUNT * PIECE, 1)
    own_total, other_total = own_ref[tail, :], other_ref[tail, :]
    later = piece_column(jnp.exp(jnp.where(mine == 0, other_total, own_total)))
    own_factor = jnp.where(mine == 0, later, 1.0)
    other_factor = jnp.where(mine == 0, 1.0, later)
    total = own_total + other_total
    for p in range(CHIP_COUNT):
        at = pl.ds(p * PIECE, PIECE)
        to = place(p, FORTH_REVERSED) * (PIECE + 1)
        out_ref[pl.ds(to, PIECE), :] = (
            own_factor * own_ref[at, :] + other_factor * other_ref[at, :]
        )
        out_ref[pl.ds(to + PIECE, 1), :] = total


def chip_states(own, other):
    return pl.pallas_call(
        chip_kernel,
        in_specs=[pl.BlockSpec(memory_space=pltpu.VMEM)] * 2,
        out_specs=[pl.BlockSpec(memory_space=pltpu.VMEM)] * 2,
        out_shape=[
            jax.ShapeDtypeStruct((CHIP_COUNT * (PIECE + 1), 128), F32),
            jax.ShapeDtypeStruct(own.shape, F32),
        ],
        input_output_aliases={0: 1},
        compiler_params=pltpu.CompilerParams(vmem_limit_bytes=8 << 20),
        cost_estimate=pl.CostEstimate(flops=1 << 19, bytes_accessed=3 << 19, transcendentals=128),
        name="chip_states",
    )(own, other)


def scan_kernel(in_ref, out_ref, final_ref, last_ref):
    state = jnp.zeros((PIECE, 128), F32)
    for p in range(CHIP_COUNT):
        out_ref[pl.ds(place(p, BACK_REVERSED) * PIECE, PIECE), :] = state
        at = place(p, FORTH_REVERSED) * (PIECE + 1)
        factor = piece_column(jnp.exp(in_ref[pl.ds(at + PIECE, 1), :]))
        state = factor * state + in_ref[pl.ds(at, PIECE), :]
    last_ref[...] = state
    for i in range(2):
        final_ref[:, i * 128 : (i + 1) * 128] = last_ref[pl.ds(i, HEADS_HERE, stride=2), :]


def scan_chips(pieces):
    return pl.pallas_call(
        scan_kernel,
        out_shape=[
            jax.ShapeDtypeStruct((CHIP_COUNT * PIECE, 128), F32),
            jax.ShapeDtypeStruct((HEADS_HERE, 2 * HEAD_DIM), F32),
        ],
        scratch_shapes=[pltpu.VMEM((PIECE, 128), F32)],
        compiler_params=pltpu.CompilerParams(vmem_limit_bytes=8 << 20),
        cost_estimate=pl.CostEstimate(flops=1 << 19, bytes_accessed=1 << 20, transcendentals=4096),
        name="scan_chips",
    )(pieces)


def inside_kernel(
    first, q_ref, k_ref, v_ref, fading_ref, pace_ref, even_ref, odd_ref, out_ref, *more
):
    *factor_ref, c_ref, column_ref = more
    g = pl.program_id(0)
    h0 = first + g * GROUP
    second = core_index() == 1

    @pl.when(g == 0)
    def _():
        c = log_decay(fading_ref[...], pace_ref[...])
        c_ref[...] = c
        column_ref[...] = to_columns(c)
        if factor_ref:
            partner = jnp.where(second, odd_ref[pl.ds(CHIP_COUNT * PIECE, 1), :], 0.0)
            factor_ref[0][...] = jnp.exp(column_ref[...] + partner)

    columns = pltpu.roll(column_ref[...], lax.rem(128 - h0, 128), axis=1)
    starts = shuffle(
        [
            jnp.stack(
                [
                    jnp.where(second, ref[pl.ds(pl.multiple_of((2 * j + b) * PIECE + 2 * h0, 8), 8), :], 0.0)
                    for j in range(16)
                ]
            )
            for b in range(2)
            for ref in (even_ref, odd_ref)
        ]
    )
    row = lax.broadcasted_iota(jnp.int32, (BLOCK, BLOCK), 0)
    col = lax.broadcasted_iota(jnp.int32, (BLOCK, BLOCK), 1)
    for i in range(GROUP):
        lanes = slice(i * HEAD_DIM, (i + 1) * HEAD_DIM)
        c_row = c_ref[pl.ds(h0 + i, 1), :]
        state = starts[i].reshape(HEAD_DIM, HEAD_DIM)
        base = jnp.zeros((1, 1), F32)
        for b in range(TOKENS_HERE // BLOCK):
            rows = slice(b * BLOCK, (b + 1) * BLOCK)
            q, k, v = q_ref[rows, lanes], k_ref[rows, lanes], v_ref[rows, lanes]
            c_here = c_row[:, rows]
            c_column = columns[rows, i : i + 1]
            diff = c_column - c_here
            factor = jnp.where(row >= col, jnp.exp(jnp.minimum(diff, 0.0)), 0.0)
            weights = (dot(q, k, ((1,), (1,))) * factor).astype(BF16)
            high, low = split(state)
            carried = dot(q, high) + dot(q, low)
            out_ref[rows, lanes] = dot(weights, v) + jnp.exp(c_column - base) * carried
            if b + 1 < TOKENS_HERE // BLOCK:
                last = c_here[:, -1:]
                decayed = k.T.astype(F32) * jnp.exp(last - c_here)
                high, low = split(decayed)
                state = jnp.exp(last - base) * state + dot(high, v) + dot(low, v)
                base = last


def inside(q, k, v, fading, pace, even, odd, first, heads, with_factor):
    at = first // GROUP
    wide = pl.BlockSpec((TOKENS_HERE, GROUP * HEAD_DIM), lambda g: (0, at + g))
    out_specs = [pl.BlockSpec((TOKENS_HERE, GROUP * HEAD_DIM), lambda g: (0, g))]
    out_shape = [jax.ShapeDtypeStruct((TOKENS_HERE, heads * HEAD_DIM), F32)]
    if with_factor:
        out_specs.append(pl.BlockSpec((TOKENS_HERE, 128), lambda g: (0, 0)))
        out_shape.append(jax.ShapeDtypeStruct((TOKENS_HERE, 128), F32))
    return pl.pallas_call(
        functools.partial(inside_kernel, first),
        grid=(heads // GROUP,),
        in_specs=[
            wide,
            wide,
            wide,
            pl.BlockSpec((HEADS_HERE, TOKENS_HERE), lambda g: (0, 0)),
            pl.BlockSpec((1, HEADS_HERE), lambda g: (0, 0)),
            pl.BlockSpec(even.shape, lambda g: (0, 0)),
            pl.BlockSpec(odd.shape, lambda g: (0, 0)),
        ],
        out_specs=out_specs,
        out_shape=out_shape,
        scratch_shapes=[
            pltpu.VMEM((HEADS_HERE, TOKENS_HERE), F32),
            pltpu.VMEM((TOKENS_HERE, 128), F32),
        ],
        compiler_params=pltpu.CompilerParams(vmem_limit_bytes=24 << 20),
        cost_estimate=pl.CostEstimate(
            flops=1_000_000_000, bytes_accessed=6 << 20, transcendentals=1 << 20
        ),
        name="inside",
    )(q, k, v, fading, pace, even, odd)


def fetch_kernel(q_hbm, own_hbm, low_hbm, q_ref, own_ref, low_ref, sems):
    first = low_hbm.at[:, pl.ds(0, GROUP * HEAD_DIM)]
    pairs = ((own_hbm, own_ref), (q_hbm, q_ref), (first, low_ref))
    copies = [
        pltpu.make_async_copy(source, target, sems.at[n])
        for n, (source, target) in enumerate(pairs)
    ]
    for copy in copies:
        copy.start()
    for copy in copies:
        copy.wait()


def fetched(q, own, before_low):
    group = (TOKENS_HERE, GROUP * HEAD_DIM)
    return pl.pallas_call(
        fetch_kernel,
        in_specs=[pl.BlockSpec(memory_space=pl.ANY)] * 3,
        out_specs=[pl.BlockSpec(memory_space=pltpu.VMEM)] * 3,
        out_shape=[
            jax.ShapeDtypeStruct(q.shape, BF16),
            jax.ShapeDtypeStruct(own.shape, F32),
            jax.ShapeDtypeStruct(group, F32),
        ],
        scratch_shapes=[pltpu.SemaphoreType.DMA((3,))],
        compiler_params=pltpu.CompilerParams(vmem_limit_bytes=8 << 20),
        cost_estimate=pl.CostEstimate(flops=0, bytes_accessed=7 << 20, transcendentals=0),
        name="fetched",
    )(q, own, before_low)


def outside_kernel(
    q_ref, own_ref, first_ref, low_hbm, high_ref, other_ref, factor_ref, out_ref, squares_ref, sum_ref, second_ref, sem
):
    second = low_hbm.at[:, pl.ds(GROUP * HEAD_DIM, GROUP * HEAD_DIM)]
    copy = pltpu.make_async_copy(second, second_ref, sem)
    copy.start()
    mine = core_index()
    width = GROUP * HEAD_DIM
    half = GROUPS // 2

    def group(g, before_ref, start):
        columns = pltpu.roll(factor_ref[...], (128 - g * GROUP) % 128, axis=1)
        rows = pl.ds(pl.multiple_of(g * 8, 8), 8)
        own, other = (
            jnp.stack([ref[place(p, BACK_REVERSED), rows, :] for p in range(CHIP_COUNT)])
            for ref in (own_ref, other_ref)
        )
        even = jnp.where(mine == 0, own, other).reshape(16, 2, 8, 128)
        odd = jnp.where(mine == 0, other, own).reshape(16, 2, 8, 128)
        states = shuffle([even[:, 0], odd[:, 0], even[:, 1], odd[:, 1]])
        total = None
        for i in range(GROUP):
            high, low_part = split(states[i].reshape(HEAD_DIM, HEAD_DIM))
            here = pl.ds(pl.multiple_of(g * width + i * HEAD_DIM, HEAD_DIM), HEAD_DIM)
            there = pl.ds(pl.multiple_of((g - start) * width + i * HEAD_DIM, HEAD_DIM), HEAD_DIM)
            q = q_ref[:, here]
            carried = dot(jnp.concatenate([q, q], axis=1), jnp.concatenate([high, low_part], axis=0))
            out = before_ref[:, there] + columns[:, i : i + 1] * carried
            out_ref[:, here] = out
            total = out * out if total is None else total + out * out
        return total

    sum_ref[...] = jnp.zeros_like(sum_ref)

    def high_group(g, carry):
        sum_ref[...] += group(g, high_ref, half)
        return carry

    lax.fori_loop(half, GROUPS, high_group, 0)
    sum_ref[...] += group(0, first_ref, 0)
    copy.wait()
    sum_ref[...] += group(1, second_ref, 1)
    squares_ref[...] = jnp.sum(sum_ref[...].T, axis=0, keepdims=True)


def outside(q, own, first, before_low, before_high, other, factor):
    here = pl.BlockSpec(memory_space=pltpu.VMEM)
    return pl.pallas_call(
        outside_kernel,
        in_specs=[here] * 3 + [pl.BlockSpec(memory_space=pl.ANY)] + [here] * 3,
        out_specs=[here, here],
        out_shape=[
            jax.ShapeDtypeStruct((TOKENS_HERE, HEADS_HERE * HEAD_DIM), F32),
            jax.ShapeDtypeStruct((1, TOKENS_HERE), F32),
        ],
        scratch_shapes=[
            pltpu.VMEM((TOKENS_HERE, 128), F32),
            pltpu.VMEM((TOKENS_HERE, GROUP * HEAD_DIM), F32),
            pltpu.SemaphoreType.DMA,
        ],
        compiler_params=pltpu.CompilerParams(vmem_limit_bytes=24 << 20),
        cost_estimate=pl.CostEstimate(
            flops=600_000_000, bytes_accessed=11 << 20, transcendentals=0
        ),
        name="outside",
    )(q, own, first, before_low, before_high, other, factor)


NORM_ROWS = 64


def norm_kernel(out_ref, *refs):
    *square_refs, gain_ref, result_hbm, column_ref, result_ref, sems = refs
    total = sum(ref[...] for ref in square_refs)
    scale = lax.rsqrt(total / D + 1e-06)
    column_ref[...] = jnp.broadcast_to(scale, (128, TOKENS_HERE)).T
    steps = TOKENS_HERE // NORM_ROWS

    def write(t):
        rows = pl.ds(pl.multiple_of(t * NORM_ROWS, NORM_ROWS), NORM_ROWS)
        return pltpu.make_async_copy(result_ref.at[rows, :], result_hbm.at[rows, :], sems.at[t])

    def step(t, carry):
        rows = pl.ds(pl.multiple_of(t * NORM_ROWS, NORM_ROWS), NORM_ROWS)
        column = column_ref[rows, :]
        for h in range(HEADS_HERE):
            lanes = slice(h * HEAD_DIM, (h + 1) * HEAD_DIM)
            result_ref[rows, lanes] = (out_ref[rows, lanes] * column * gain_ref[:, lanes]).astype(BF16)
        write(t).start()
        return carry

    def finish(t, carry):
        write(t).wait()
        return carry

    lax.fori_loop(0, steps, step, 0)
    lax.fori_loop(0, steps, finish, 0)


def normed(out, squares, gain):
    width = HEADS_HERE * HEAD_DIM
    here = pl.BlockSpec(memory_space=pltpu.VMEM)
    return pl.pallas_call(
        norm_kernel,
        in_specs=[here] * (2 + len(squares)),
        out_specs=pl.BlockSpec(memory_space=pl.ANY),
        out_shape=jax.ShapeDtypeStruct((TOKENS_HERE, width), BF16),
        scratch_shapes=[
            pltpu.VMEM((TOKENS_HERE, 128), F32),
            pltpu.VMEM((TOKENS_HERE, width), BF16),
            pltpu.SemaphoreType.DMA((TOKENS_HERE // NORM_ROWS,)),
        ],
        compiler_params=pltpu.CompilerParams(vmem_limit_bytes=24 << 20),
        cost_estimate=pl.CostEstimate(flops=1 << 21, bytes_accessed=6 << 20, transcendentals=512),
        name="normed",
    )(out, *squares, gain)


def turned(value, by):
    count = lax.axis_size("tp")
    return lax.ppermute(value, "tp", [((i + by) % count, i) for i in range(count)])


def layer(q, k, v, pace, fading, gain):
    q, k, v, fading, pace = (
        pltpu.with_memory_space_constraint(part, pltpu.HBM)
        for part in (q, k, v, fading.T, pace.reshape(1, HEADS_HERE))
    )
    keep, send = local_states(k, v, fading, pace)
    swap = [(i, i ^ 1) for i in range(SHARDS)]
    received = lax.ppermute(send, SEQ, swap)
    chip, kept = chip_states(keep, received)
    partner = lax.ppermute(kept, SEQ, swap)
    gathered = lax.all_to_all(
        chip.reshape(CHIP_COUNT, PIECE + 1, 1, 128),
        SEQ,
        0,
        0,
        axis_index_groups=groups(FORTH_REVERSED),
        tiled=True,
    )
    half = HEADS_HERE // 2
    arguments = (q, k, v, fading, pace, partner, received)
    before_low, factor = inside(*arguments, 0, half, True)
    before_low = pltpu.with_memory_space_constraint(before_low, pltpu.HBM)
    prior, final = scan_chips(gathered.reshape(CHIP_COUNT * (PIECE + 1), 128))
    own = lax.all_to_all(
        prior.reshape(CHIP_COUNT, PIECE, 128),
        SEQ,
        0,
        0,
        axis_index_groups=groups(BACK_REVERSED),
        tiled=True,
    )
    (before_high,) = inside(*arguments, half, half, False)
    other = lax.ppermute(own, SEQ, swap)
    near = fetched(q, own, before_low)
    out, squares = outside(*near, before_low, before_high, other, factor)
    squares = [squares, *(turned(squares, by) for by in (1, 3, 2))]
    return normed(out, squares, gain.reshape(1, -1)), final


def solution(mesh):
    return jax.shard_map(
        layer,
        mesh=mesh,
        in_specs=(P(SEQ, "tp"), P(SEQ, "tp"), P(SEQ, "tp"), P("tp"), P(SEQ, "tp"), P("tp")),
        out_specs=(P(SEQ, "tp"), P("tp", SEQ)),
        check_vma=False,
    )
```
